128 devices in a mesh: front: 4 (over y), rows: 32 (over z, x, core).
Axes of the slice: x: 4, y: 4, z: 4, core: 2. Of those that a mesh axis runs over, the one named last changes fastest.
Arguments:
- panel_g: bfloat16 [4, 32, 2048, 256], P('front', 'rows'), may hold values from -6 to 6
- refl_root: bfloat16 [4, 32, 2048, 512], P('front', 'rows'), may hold values from -6 to 6
- refl_mid: bfloat16 [4, 32, 4096, 512], P('front', 'rows'), may hold values from -6 to 6
- refl_leaf: bfloat16 [4, 32, 4096, 512], P('front', 'rows'), may hold values from -6 to 6
- tri_root: float32 [512, 512], replicated, as said below
- tri_mid: float32 [4, 512, 512], P('front'), as said below
- tri_leaf: float32 [4, 512, 512], P('front'), as said below
- route_root: int32 [4, 32, 16], P('front', 'rows'), may hold values from 0 to 3, as said below
- route_mid: int32 [4, 32, 32], P('front', 'rows'), may hold values from 0 to 3, as said below
Outputs:
- leaf_g: bfloat16 [4, 32, 4096, 256], P('front', 'rows')
The draws below stay inside these ranges and needn't reach their ends.
Inputs may be any that keep to these rules, and one draw needn't show every extreme that they name: `route_root`: on every device at most 8 blocks name the same front, and some front is named by exactly 8 of them. `route_mid`: on every device each front is named by exactly 8 slots. `tri_root`: upper triangular. `tri_mid`: upper triangular. `tri_leaf`: upper triangular.
All inputs are finite; a program needn't handle non-finite values.
Results may differ from the reference program's by a relative error of at most 0.01.
Values may be sent and summed in bfloat16 or wider, within the bound.
No kernel may reach another device: no remote copies, remote signals or barrier semaphores. Data moves between devices by JAX's collectives and lax.ppermute only.
A program may use at most 64 MiB of HBM per device.

```python
import math
import jax
import jax.numpy as jnp
from jax import lax

K = 512
R = 256
BLOCK = 128
BLK_DEV = 16
SLOTS = 32
N_FRONT = 4
N_ROWS = 32


def root_targets(device_key):
    first_key, second_key, third_key = jax.random.split(device_key, 3)
    capacity = BLK_DEV // 2
    leading = jax.random.randint(first_key, (), 0, N_FRONT)
    others = (leading + 1 + jnp.arange((N_FRONT - 1) * capacity) // capacity) % N_FRONT
    chosen = jax.random.permutation(second_key, others)[:capacity]
    combined = jnp.concatenate([jnp.full((capacity,), leading), chosen])
    return jax.random.permutation(third_key, combined).astype(jnp.int32)


def draw_route_root(key, part):
    device_keys = jax.random.split(jax.random.fold_in(key, 11), N_FRONT * N_ROWS)
    return jax.vmap(root_targets)(device_keys).reshape(N_FRONT, N_ROWS, BLK_DEV)


def mid_targets(device_key):
    capacity = BLK_DEV // 2
    return jax.random.permutation(device_key, jnp.arange(N_FRONT * capacity) // capacity).astype(jnp.int32)


def draw_route_mid(key, part):
    device_keys = jax.random.split(jax.random.fold_in(key, 23), N_FRONT * N_ROWS)
    return jax.vmap(mid_targets)(device_keys).reshape(N_FRONT, N_ROWS, N_FRONT * (BLK_DEV // 2))


def triangles(base_key, count, front_rows):
    diag_key, upper_key = jax.random.split(base_key)
    diagonal = jnp.exp(jax.random.uniform(diag_key, (count, K), jnp.float32, math.log(0.5), math.log(1.5)))
    upper = 0.7 * jax.random.normal(upper_key, (count, K, K), jnp.float32)
    identity = jnp.eye(K, dtype=jnp.float32)
    result = identity[None, :, :] * diagonal[:, None, :] + jnp.triu(upper, 1) / math.sqrt(K)
    return (result / math.sqrt(K * front_rows)).astype(jnp.float32)


def draw_tri_root(key, part):
    return triangles(jax.random.fold_in(key, 31), 1, N_FRONT * N_ROWS * BLK_DEV * BLOCK)[0]


def draw_tri_mid(key, part):
    return triangles(jax.random.fold_in(key, 37), N_FRONT, N_ROWS * BLK_DEV * BLOCK)


def draw_tri_leaf(key, part):
    return triangles(jax.random.fold_in(key, 41), N_FRONT, N_ROWS * BLK_DEV * BLOCK)


def shard_levels(own_key, shape, pieces, least, top_value):
    factor_of = 1.0
    for axis_at, parts in pieces:
        steps = jax.random.uniform(jax.random.fold_in(jax.random.fold_in(own_key, 6), axis_at), (parts,), jnp.float32, least / len(pieces), top_value / len(pieces))
        factor_of = factor_of * jnp.repeat(jnp.exp(steps), shape[axis_at] // parts).reshape((-1,) + (1,) * (len(shape) - 1 - axis_at))
    return factor_of


def centred(stream_key, extent, deviation, reach, shards=(), kind=jnp.bfloat16):
    drawn = deviation * jax.random.normal(stream_key, extent, jnp.float32)
    if shards:
        drawn = drawn * shard_levels(stream_key, extent, shards, -0.22, 0.18)
    return jnp.clip(drawn, -reach, reach).astype(kind)


def setup_inputs(seed: int = 0) -> dict:
    streams_of = jax.random.split(jax.random.key(seed), 10)
    panel_g = centred(streams_of[0], (N_FRONT, N_ROWS, BLK_DEV * BLOCK, R), 1.0, 6.0, ((0, 4), (1, 32)))
    refl_root = centred(streams_of[1], (N_FRONT, N_ROWS, BLK_DEV * BLOCK, K), 1.0, 6.0, ((0, 4), (1, 32)))
    refl_mid = centred(streams_of[2], (N_FRONT, N_ROWS, SLOTS * BLOCK, K), 1.0, 6.0, ((0, 4), (1, 32)))
    refl_leaf = centred(streams_of[3], (N_FRONT, N_ROWS, SLOTS * BLOCK, K), 1.0, 6.0, ((0, 4), (1, 32)))
    tri_root = draw_tri_root(jax.random.fold_in(streams_of[9], 71), 0)
    tri_mid = draw_tri_mid(jax.random.fold_in(streams_of[9], 71), 0)
    tri_leaf = draw_tri_leaf(jax.random.fold_in(streams_of[9], 71), 0)
    route_root = draw_route_root(jax.random.fold_in(streams_of[9], 71), 0)
    route_mid = draw_route_mid(jax.random.fold_in(streams_of[9], 71), 0)
    return dict(panel_g=panel_g, refl_root=refl_root, refl_mid=refl_mid, refl_leaf=refl_leaf, tri_root=tri_root, tri_mid=tri_mid, tri_leaf=tri_leaf, route_root=route_root, route_mid=route_mid)


def reflect(panel_g, reflectors, triangle, live_rows):
    width_k = reflectors.shape[-1]
    flat_refl = reflectors.reshape(-1, width_k)
    flat_panel = panel_g.reshape(-1, panel_g.shape[-1])
    summed = lax.dot_general(flat_refl, flat_panel, (((0,), (0,)), ((), ())), preferred_element_type=jnp.float32)
    coeffs = jnp.dot(triangle.T, summed, precision=lax.Precision.HIGHEST, preferred_element_type=jnp.float32).astype(jnp.bfloat16)
    update = jnp.dot(flat_refl, coeffs, preferred_element_type=jnp.float32)
    result = (flat_panel.astype(jnp.float32) - update) * live_rows.reshape(-1, 1)
    return result.astype(jnp.bfloat16).reshape(panel_g.shape)


def placement(targets, front_count, capacity):
    onehot = (targets[..., None] == jnp.arange(front_count, dtype=jnp.int32)).astype(jnp.int32)
    before = jnp.cumsum(onehot, axis=-2) - onehot
    position = jnp.sum(before * onehot, axis=-1)
    slot_index = targets * capacity + position
    return (slot_index[..., None, :] == jnp.arange(front_count * capacity, dtype=jnp.int32)[:, None]).astype(jnp.float32)


def route(panel_g, live_blocks, targets, capacity):
    front_count = panel_g.shape[0]
    rows_count = panel_g.shape[1]
    block_count = targets.shape[-1]
    selector = placement(targets, front_count, capacity)
    blocks = panel_g.reshape(front_count, rows_count, block_count, -1)

    def one_front(members):
        chooser, grouped = members
        return jnp.einsum("rsb,rbx->rsx", chooser, grouped.astype(jnp.float32)).astype(jnp.bfloat16)

    outgoing = lax.map(one_front, (selector, blocks))
    filled = jnp.einsum("frsb,frb->frs", selector, live_blocks)
    outgoing = outgoing.reshape(front_count, rows_count, front_count, capacity, -1).transpose(2, 1, 0, 3, 4)
    filled = filled.reshape(front_count, rows_count, front_count, capacity).transpose(2, 1, 0, 3)
    slot_count = front_count * capacity
    moved_rows = outgoing.reshape(front_count, rows_count, slot_count * BLOCK, panel_g.shape[-1])
    return moved_rows, filled.reshape(front_count, rows_count, slot_count)


def per_front(members):
    return reflect(*members)


def reference(panel_g, refl_root, refl_mid, refl_leaf, tri_root, tri_mid, tri_leaf, route_root, route_mid):
    root_live = jnp.ones(panel_g.shape[:3], jnp.float32)
    level_one = reflect(panel_g, refl_root, tri_root, root_live)
    moved_rows, filled = route(level_one, jnp.ones(route_root.shape, jnp.float32), route_root, BLK_DEV // 2)
    live_rows = jnp.repeat(filled, BLOCK, axis=2)
    level_two = lax.map(per_front, (moved_rows, refl_mid, tri_mid, live_rows))
    moved_rows, filled = route(level_two, filled, route_mid, BLK_DEV // 2)
    live_rows = jnp.repeat(filled, BLOCK, axis=2)
    return lax.map(per_front, (moved_rows, refl_leaf, tri_leaf, live_rows))
```

```python
import jax
import jax.numpy as jnp
from jax import lax
from jax.experimental import pallas as pl
from jax.experimental.pallas import tpu as pltpu
from jax.sharding import Mesh
from jax.sharding import PartitionSpec as P

BLOCK = 128
FRONTS = 4
CAP = 8
COLS = 256
REFL = 512
CHUNK = CAP * BLOCK
TILE = 512
ROWS = ("rows_0", "rows_1", "rows_2")
ALL = ("front",) + ROWS
F32 = jnp.float32
BF16 = jnp.bfloat16


def row_sums(panel, refl):
    return lax.dot_general(panel, refl, (((0,), (0,)), ((), ())), preferred_element_type=F32)


def times_coeffs(refl, coeffs_t):
    return lax.dot_general(refl, coeffs_t, (((1,), (1,)), ((), ())), preferred_element_type=F32)


def root_partial(panel, refl):
    steps = panel.shape[0] // TILE

    def kernel(g_ref, y_ref, out_ref, acc_ref):
        i = pl.program_id(0)
        part = row_sums(g_ref[...], y_ref[...])

        @pl.when(i == 0)
        def _():
            acc_ref[...] = part

        @pl.when(i > 0)
        def _():
            acc_ref[...] += part

        @pl.when(i == steps - 1)
        def _():
            for j in range(4):
                out_ref[pl.ds(j, COLS, stride=4), :] = acc_ref[:, 128 * j : 128 * (j + 1)]

    return pl.pallas_call(
        kernel,
        grid=(steps,),
        in_specs=[
            pl.BlockSpec((TILE, COLS), lambda i: (i, 0)),
            pl.BlockSpec((TILE, REFL), lambda i: (i, 0)),
        ],
        out_specs=pl.BlockSpec((COLS * 4, 128), lambda i: (0, 0)),
        out_shape=jax.ShapeDtypeStruct((COLS * 4, 128), F32),
        scratch_shapes=[pltpu.VMEM((COLS, REFL), F32)],
        name="root_partial",
    )(panel, refl)


def front_partial(panel, refl, source, acc):
    steps = panel.shape[0] // TILE
    has_acc = acc is not None

    def kernel(src_ref, g_ref, y_ref, *rest):
        out_ref = rest[-1]
        i = pl.program_id(0)
        part = row_sums(g_ref[...], y_ref[...])

        @pl.when(i == 0)
        def _():
            out_ref[...] = part + rest[0][...] if has_acc else part

        @pl.when(i > 0)
        def _():
            out_ref[...] += part

    whole = pl.BlockSpec((COLS, REFL), lambda i, s: (0, 0))
    return pl.pallas_call(
        kernel,
        grid_spec=pltpu.PrefetchScalarGridSpec(
            num_scalar_prefetch=1,
            grid=(steps,),
            in_specs=[
                pl.BlockSpec((TILE, COLS), lambda i, s: (i, 0)),
                pl.BlockSpec((TILE, REFL), lambda i, s: (s[0] * steps + i, 0)),
            ]
            + ([whole] if has_acc else []),
            out_specs=whole,
        ),
        out_shape=jax.ShapeDtypeStruct((COLS, REFL), F32),
        name="front_partial",
    )(source, panel, refl, *([acc] if has_acc else []))


def split_bf16(x):
    high = x.astype(BF16)
    return high, (x - high.astype(F32)).astype(BF16)


def fine_dot(a, b):
    a_high, a_low = split_bf16(a)
    b_high, b_low = split_bf16(b)
    dot = lambda u, v: jnp.dot(u, v, preferred_element_type=F32)
    return dot(a_high, b_high) + (dot(a_low, b_high) + dot(a_high, b_low))


def root_share(arrived, triangle):
    count = arrived.shape[0]

    def kernel(x_ref, t_ref, out_ref):
        total = jnp.sum(x_ref[...], axis=0)
        rows = [jnp.concatenate([total[4 * c + j : 4 * c + j + 1] for j in range(4)], 1) for c in range(2)]
        both = jnp.concatenate(rows + [jnp.zeros((6, REFL), F32)], axis=0)
        coeffs = fine_dot(both, t_ref[...]).astype(BF16).astype(F32)
        chunk = jnp.concatenate(
            [coeffs[c : c + 1, 128 * j : 128 * (j + 1)] for c in range(2) for j in range(4)], 0
        )
        out_ref[...] = jnp.broadcast_to(chunk[None], out_ref.shape)

    return pl.pallas_call(
        kernel,
        out_shape=jax.ShapeDtypeStruct((count, 8, 128), F32),
        name="root_share",
    )(arrived, triangle)


def front_share(arrived, triangle):
    def kernel(x_ref, t_ref, out_ref):
        total = jnp.sum(x_ref[...], axis=0)
        coeffs = fine_dot(total, t_ref[...]).astype(BF16)
        out_ref[...] = jnp.broadcast_to(coeffs[None], out_ref.shape)

    return pl.pallas_call(
        kernel,
        out_shape=jax.ShapeDtypeStruct(arrived.shape, BF16),
        name="front_share",
    )(arrived, triangle)


def scatter_blocks(table_ref, scratch_ref, out_refs, limit):
    for d in range(FRONTS):
        for p in range(CAP):
            at = table_ref[d * CAP + p]
            start = pl.multiple_of(jnp.clip(at, 0, limit - 1) * BLOCK, BLOCK)
            block = scratch_ref[pl.ds(start, BLOCK), :]
            out_refs[d][p * BLOCK : (p + 1) * BLOCK, :] = jnp.where(at >= 0, block, jnp.zeros_like(block))


def root_apply(coeffs, panel, refl, table):
    steps = panel.shape[0] // TILE
    blocks = panel.shape[0] // BLOCK

    def kernel(t_ref, c_ref, g_ref, y_ref, o0, o1, o2, o3, ct_ref, new_ref):
        i = pl.program_id(0)

        @pl.when(i == 0)
        def _():
            for j in range(4):
                ct_ref[:, 128 * j : 128 * (j + 1)] = c_ref[pl.ds(j, COLS, stride=4), :].astype(BF16)

        new = g_ref[...].astype(F32) - times_coeffs(y_ref[...], ct_ref[...])
        new_ref[pl.ds(pl.multiple_of(i * TILE, TILE), TILE), :] = new.astype(BF16)

        @pl.when(i == steps - 1)
        def _():
            scatter_blocks(t_ref, new_ref, (o0, o1, o2, o3), blocks)

    out = pl.BlockSpec((CHUNK, COLS), lambda i, t: (0, 0))
    return pl.pallas_call(
        kernel,
        grid_spec=pltpu.PrefetchScalarGridSpec(
            num_scalar_prefetch=1,
            grid=(steps,),
            in_specs=[
                pl.BlockSpec((COLS * 4, 128), lambda i, t: (0, 0)),
                pl.BlockSpec((TILE, COLS), lambda i, t: (i, 0)),
                pl.BlockSpec((TILE, REFL), lambda i, t: (i, 0)),
            ],
            out_specs=[out] * FRONTS,
            scratch_shapes=[pltpu.VMEM((COLS, REFL), BF16), pltpu.VMEM(panel.shape, BF16)],
        ),
        out_shape=[jax.ShapeDtypeStruct((CHUNK, COLS), BF16)] * FRONTS,
        name="root_apply",
    )(table, coeffs, panel, refl)


def updated_tile(i, per, live_ref, c_ref, g_refs, y_ref, write):
    update = times_coeffs(y_ref[...], c_ref[...])
    for d in range(FRONTS):

        @pl.when(i // per == d)
        def _():
            for b in range(TILE // BLOCK):
                live = live_ref[i * (TILE // BLOCK) + b]
                at = slice(b * BLOCK, (b + 1) * BLOCK)
                new = g_refs[d][at, :].astype(F32) - update[at, :]
                write(b, jnp.where(live > 0, new, jnp.zeros_like(new)).astype(BF16))


def panel_spec(d, per):
    return pl.BlockSpec((TILE, COLS), lambda i, *_: (jnp.clip(i - d * per, 0, per - 1), 0))


def front_apply(coeffs, panels, refl, sources, live, table):
    per = CHUNK // TILE
    steps = FRONTS * per
    blocks = FRONTS * CAP

    def kernel(s_ref, l_ref, t_ref, c_ref, g0, g1, g2, g3, y_ref, o0, o1, o2, o3, new_ref):
        i = pl.program_id(0)

        def write(b, value):
            new_ref[pl.ds(pl.multiple_of(i * TILE + b * BLOCK, BLOCK), BLOCK), :] = value

        updated_tile(i, per, l_ref, c_ref, (g0, g1, g2, g3), y_ref, write)

        @pl.when(i == steps - 1)
        def _():
            scatter_blocks(t_ref, new_ref, (o0, o1, o2, o3), blocks)

    out = pl.BlockSpec((CHUNK, COLS), lambda i, *_: (0, 0))
    return pl.pallas_call(
        kernel,
        grid_spec=pltpu.PrefetchScalarGridSpec(
            num_scalar_prefetch=3,
            grid=(steps,),
            in_specs=[pl.BlockSpec((COLS, REFL), lambda i, *_: (0, 0))]
            + [panel_spec(d, per) for d in range(FRONTS)]
            + [pl.BlockSpec((TILE, REFL), lambda i, s, *_: (s[i // per] * per + i % per, 0))],
            out_specs=[out] * FRONTS,
            scratch_shapes=[pltpu.VMEM((FRONTS * CHUNK, COLS), BF16)],
        ),
        out_shape=[jax.ShapeDtypeStruct((CHUNK, COLS), BF16)] * FRONTS,
        name="front_apply",
    )(sources, live, table, coeffs, *panels, refl)


def leaf_apply(coeffs, panels, refl, sources, live):
    per = CHUNK // TILE
    steps = FRONTS * per

    def kernel(s_ref, l_ref, c_ref, g0, g1, g2, g3, y_ref, out_ref):
        i = pl.program_id(0)

        def write(b, value):
            out_ref[b * BLOCK : (b + 1) * BLOCK, :] = value

        updated_tile(i, per, l_ref, c_ref, (g0, g1, g2, g3), y_ref, write)

    return pl.pallas_call(
        kernel,
        grid_spec=pltpu.PrefetchScalarGridSpec(
            num_scalar_prefetch=2,
            grid=(steps,),
            in_specs=[pl.BlockSpec((COLS, REFL), lambda i, *_: (0, 0))]
            + [panel_spec(d, per) for d in range(FRONTS)]
            + [pl.BlockSpec((TILE, REFL), lambda i, s, *_: (s[i // per] * per + i % per, 0))],
            out_specs=pl.BlockSpec((TILE, COLS), lambda i, s, *_: (s[i // per] * per + i % per, 0)),
        ),
        out_shape=jax.ShapeDtypeStruct((FRONTS * CHUNK, COLS), BF16),
        name="leaf_apply",
    )(sources, live, coeffs, *panels, refl)


def shifted(x, d):
    return x if d == 0 else lax.ppermute(x, "front", [(i, (i + d) % FRONTS) for i in range(FRONTS)])


def exchange(outgoing):
    arrived = {d: shifted(outgoing[d], d) for d in (2, 1, 3, 0)}
    return [arrived[d] for d in range(FRONTS)]


def ranks(targets):
    at = jnp.arange(targets.shape[-1], dtype=jnp.int32)
    same = targets[..., :, None] == targets[..., None, :]
    return jnp.sum((same & (at[:, None] > at[None, :])).astype(jnp.int32), axis=-1)


def all_to_all(x, axes):
    return lax.all_to_all(x, axes, 0, 0, tiled=True)


def tables(route_root, route_mid):
    me = lax.axis_index("front")
    shifts = jnp.arange(FRONTS, dtype=jnp.int32)
    sources = (me - shifts) % FRONTS
    places = jnp.arange(CAP, dtype=jnp.int32)
    goal = jnp.repeat((me + shifts) % FRONTS, CAP)
    spot = jnp.tile(places, FRONTS)

    def picked(targets):
        hit = (targets[None, :] == goal[:, None]) & (ranks(targets)[None, :] == spot[:, None])
        at = jnp.arange(targets.shape[0], dtype=jnp.int32)
        return jnp.sum(jnp.where(hit, at[None, :] + 1, 0), axis=1) - 1

    root_table = picked(route_root)
    slots = picked(route_mid)
    mid_table = ((me - slots // CAP) % FRONTS) * CAP + slots % CAP

    own = jnp.concatenate([route_root, route_mid])
    every = jnp.stack([shifted(own, d) for d in range(FRONTS)])
    roots, mids = every[:, : route_root.shape[0]], every[:, route_root.shape[0] :]
    counts = jnp.sum((roots[:, None, :] == sources[None, :, None]).astype(jnp.int32), axis=-1)
    live_mid = (places[None, :] < counts[:, :1]).astype(jnp.int32).reshape(-1)
    order = (sources[None, :] == shifts[:, None]).astype(jnp.int32)
    by_front = jnp.sum(order[:, :, None] * counts[None, :, :], axis=1)
    flags = (places[None, None, :] < by_front.T[:, :, None]).astype(jnp.int32).reshape(FRONTS, -1)
    hit = (mids == me) & (flags > 0)
    mine = hit[:, None, :] & (ranks(mids)[:, None, :] == places[None, :, None])
    live_leaf = jnp.sum(mine.astype(jnp.int32), axis=-1).reshape(-1)
    return sources, root_table, mid_table, live_mid, live_leaf


def front_level(panels, refl, triangle, sources):
    acc = None
    for d in (0, 1, 3, 2):
        acc = front_partial(panels[d], refl, sources[d : d + 1], acc)
    arrived = all_to_all(acc.reshape(32, COLS // 32, REFL), ROWS)
    return all_to_all(front_share(arrived, triangle), ROWS).reshape(COLS, REFL)


def per_device(
    panel_g, refl_root, refl_mid, refl_leaf, tri_root, tri_mid, tri_leaf, route_root, route_mid
):
    panel = panel_g.reshape(-1, COLS)
    y_root, y_mid, y_leaf = (y.reshape(-1, REFL) for y in (refl_root, refl_mid, refl_leaf))

    partial = root_partial(panel, y_root)
    arrived = all_to_all(partial.reshape(128, 8, 128), ALL)
    coeffs = all_to_all(root_share(arrived, tri_root), ALL).reshape(COLS * 4, 128)
    sources, root_table, mid_table, live_mid, live_leaf = tables(
        route_root.reshape(-1), route_mid.reshape(-1)
    )
    panels = exchange(root_apply(coeffs, panel, y_root, root_table))

    coeffs = front_level(panels, y_mid, tri_mid[0], sources)
    panels = exchange(front_apply(coeffs, panels, y_mid, sources, live_mid, mid_table))

    coeffs = front_level(panels, y_leaf, tri_leaf[0], sources)
    out = leaf_apply(coeffs, panels, y_leaf, sources, live_leaf)
    return out.reshape(refl_leaf.shape[:3] + (COLS,))


def solution(mesh):
    finer = Mesh(
        mesh.devices.reshape(mesh.shape["front"], 4, 4, 2), ("front", "rows_0", "rows_1", "rows_2")
    )
    rows = P("front", ROWS, None, None)
    placed = (
        rows,
        rows,
        rows,
        rows,
        P(),
        P("front", None, None),
        P("front", None, None),
        P("front", ROWS, None),
        P("front", ROWS, None),
    )
    return jax.shard_map(
        per_device,
        mesh=finer,
        in_specs=placed,
        out_specs=rows,
        check_vma=False,
    )
```

```python
import jax
import jax.numpy as jnp
from jax import lax
from jax.experimental import pallas as pl
from jax.experimental.pallas import tpu as pltpu
from jax.sharding import Mesh
from jax.sharding import PartitionSpec as P

BLOCK = 128
FRONTS = 4
CAP = 8
COLS = 256
REFL = 512
CHUNK = CAP * BLOCK
TILE = 512
ROWS = ("rows_0", "rows_1", "rows_2")
ALL = ("front",) + ROWS
F32 = jnp.float32
BF16 = jnp.bfloat16


def row_sums(panel, refl):
    return lax.dot_general(panel, refl, (((0,), (0,)), ((), ())), preferred_element_type=F32)


def times_coeffs(refl, coeffs_t):
    return lax.dot_general(refl, coeffs_t, (((1,), (1,)), ((), ())), preferred_element_type=F32)


VMEM = pl.BlockSpec(memory_space=pltpu.VMEM)
SMEM = pl.BlockSpec(memory_space=pltpu.SMEM)


def vmem_call(kernel, name, out_shapes, arrays, numbers=(), scratch=()):
    held = [pltpu.with_memory_space_constraint(a, pltpu.VMEM) for a in arrays]
    many = isinstance(out_shapes, list)
    outs = [pltpu.VMEM(*o) for o in (out_shapes if many else [out_shapes])]
    return pl.pallas_call(
        kernel,
        in_specs=[SMEM] * len(numbers) + [VMEM] * len(held),
        out_specs=[VMEM] * len(outs) if many else VMEM,
        out_shape=outs if many else outs[0],
        scratch_shapes=list(scratch),
        compiler_params=pltpu.CompilerParams(vmem_limit_bytes=12 << 20),
        name=name,
    )(*numbers, *held)


def rows_at(block, count=1):
    return pl.ds(pl.multiple_of(block * BLOCK, BLOCK), count * BLOCK)


def root_partial(panel, refl):
    def kernel(g_ref, y_ref, out_ref, tall_ref):
        total = row_sums(g_ref[...], y_ref[...])
        for j in range(4):
            tall_ref[pl.ds(j, COLS, stride=4), :] = total[:, 128 * j : 128 * (j + 1)]
        out_ref[...] = tall_ref[...].astype(BF16)

    scratch = [pltpu.VMEM((COLS * 4, 128), F32)]
    return vmem_call(kernel, "root_partial", ((COLS * 4, 128), BF16), [panel, refl], (), scratch)


def front_partial(panels, refl, sources):
    def kernel(s_ref, g0, g1, g2, g3, y_ref, out_ref, acc_ref):
        for d, g_ref in enumerate((g0, g1, g2, g3)):
            part = row_sums(g_ref[...], y_ref[rows_at(s_ref[d] * CAP, CAP), :])
            acc_ref[...] = part if d == 0 else acc_ref[...] + part
        out_ref[...] = acc_ref[...].astype(BF16)

    scratch = [pltpu.VMEM((COLS, REFL), F32)]
    return vmem_call(
        kernel, "front_partial", ((COLS, REFL), BF16), [*panels, refl], (sources,), scratch
    )


def split_bf16(x):
    high = x.astype(BF16)
    return high, (x - high.astype(F32)).astype(BF16)


def fine_dot(a, b):
    a_high, a_low = split_bf16(a)
    b_high, b_low = split_bf16(b)
    dot = lambda u, v: jnp.dot(u, v, preferred_element_type=F32)
    return dot(a_high, b_high) + (dot(a_low, b_high) + dot(a_high, b_low))


def root_share(arrived, triangle):
    def kernel(x_ref, t_ref, out_ref):
        total = jnp.sum(x_ref[...].astype(F32), axis=0)
        rows = [jnp.concatenate([total[4 * c + j : 4 * c + j + 1] for j in range(4)], 1) for c in range(2)]
        both = jnp.concatenate(rows + [jnp.zeros((6, REFL), F32)], axis=0)
        coeffs = fine_dot(both, t_ref[...])
        chunk = jnp.concatenate(
            [coeffs[c : c + 1, 128 * j : 128 * (j + 1)] for c in range(2) for j in range(4)], 0
        )
        out_ref[...] = jnp.broadcast_to(chunk.astype(BF16)[None], out_ref.shape)

    return vmem_call(kernel, "root_share", (arrived.shape, BF16), [arrived, triangle])


def front_share(arrived, triangle):
    def kernel(x_ref, t_ref, out_ref):
        total = jnp.sum(x_ref[...].astype(F32), axis=0)
        coeffs = fine_dot(total, t_ref[...]).astype(BF16)
        out_ref[...] = jnp.broadcast_to(coeffs[None], out_ref.shape)

    return vmem_call(kernel, "front_share", (arrived.shape, BF16), [arrived, triangle])


def scatter_blocks(table_ref, new_ref, out_refs, limit):
    for d in range(FRONTS):
        for p in range(CAP):
            at = table_ref[d * CAP + p]
            block = new_ref[rows_at(jnp.clip(at, 0, limit - 1)), :]
            out_refs[d][p * BLOCK : (p + 1) * BLOCK, :] = jnp.where(at >= 0, block, jnp.zeros_like(block))


CHUNKS = [((CHUNK, COLS), BF16)] * FRONTS


def root_apply(coeffs, panel, refl, table):
    blocks = panel.shape[0] // BLOCK

    def kernel(t_ref, c_ref, g_ref, y_ref, o0, o1, o2, o3, tall_ref, ct_ref, new_ref):
        tall_ref[...] = c_ref[...].astype(F32)
        for j in range(4):
            ct_ref[:, 128 * j : 128 * (j + 1)] = tall_ref[pl.ds(j, COLS, stride=4), :].astype(BF16)
        for i in range(blocks * BLOCK // TILE):
            at = slice(i * TILE, (i + 1) * TILE)
            new = g_ref[at, :].astype(F32) - times_coeffs(y_ref[at, :], ct_ref[...])
            new_ref[at, :] = new.astype(BF16)
        scatter_blocks(t_ref, new_ref, (o0, o1, o2, o3), blocks)

    scratch = [
        pltpu.VMEM((COLS * 4, 128), F32),
        pltpu.VMEM((COLS, REFL), BF16),
        pltpu.VMEM(panel.shape, BF16),
    ]
    return vmem_call(kernel, "root_apply", CHUNKS, [coeffs, panel, refl], (table,), scratch)


def updated(source_ref, live_ref, c_ref, g_refs, y_ref, write):
    per = TILE // BLOCK
    for d in range(FRONTS):
        for i in range(CAP // per):
            first = source_ref[d] * CAP + i * per
            update = times_coeffs(y_ref[rows_at(first, per), :], c_ref[...])
            for b in range(per):
                live = live_ref[d * CAP + i * per + b]
                old = g_refs[d][(i * per + b) * BLOCK : (i * per + b + 1) * BLOCK, :]
                new = old.astype(F32) - update[b * BLOCK : (b + 1) * BLOCK, :]
                write(d * CAP + i * per + b, first + b, jnp.where(live > 0, new, 0.0).astype(BF16))


def front_apply(coeffs, panels, refl, sources, live, table):
    def kernel(s_ref, l_ref, t_ref, c_ref, g0, g1, g2, g3, y_ref, o0, o1, o2, o3, new_ref):
        def write(place, slot, value):
            new_ref[place * BLOCK : (place + 1) * BLOCK, :] = value

        updated(s_ref, l_ref, c_ref, (g0, g1, g2, g3), y_ref, write)
        scatter_blocks(t_ref, new_ref, (o0, o1, o2, o3), FRONTS * CAP)

    scratch = [pltpu.VMEM((FRONTS * CHUNK, COLS), BF16)]
    return vmem_call(
        kernel, "front_apply", CHUNKS, [coeffs, *panels, refl], (sources, live, table), scratch
    )


def leaf_apply(coeffs, panels, refl, sources, live):
    def kernel(s_ref, l_ref, c_ref, g0, g1, g2, g3, y_ref, out_ref):
        def write(place, slot, value):
            out_ref[rows_at(slot), :] = value

        updated(s_ref, l_ref, c_ref, (g0, g1, g2, g3), y_ref, write)

    return vmem_call(
        kernel,
        "leaf_apply",
        ((FRONTS * CHUNK, COLS), BF16),
        [coeffs, *panels, refl],
        (sources, live),
    )


def shifted(x, d):
    return x if d == 0 else lax.ppermute(x, "front", [(i, (i + d) % FRONTS) for i in range(FRONTS)])


def exchange(outgoing):
    arrived = {d: shifted(outgoing[d], d) for d in (2, 1, 3, 0)}
    return [arrived[d] for d in range(FRONTS)]


def ranks(targets):
    at = jnp.arange(targets.shape[-1], dtype=jnp.int32)
    same = targets[..., :, None] == targets[..., None, :]
    return jnp.sum((same & (at[:, None] > at[None, :])).astype(jnp.int32), axis=-1)


def all_to_all(x, axes):
    return lax.all_to_all(x, axes, 0, 0, tiled=True)


def tables(route_root, route_mid):
    me = lax.axis_index("front")
    shifts = jnp.arange(FRONTS, dtype=jnp.int32)
    sources = (me - shifts) % FRONTS
    places = jnp.arange(CAP, dtype=jnp.int32)
    goal = jnp.repeat((me + shifts) % FRONTS, CAP)
    spot = jnp.tile(places, FRONTS)

    def picked(targets):
        hit = (targets[None, :] == goal[:, None]) & (ranks(targets)[None, :] == spot[:, None])
        at = jnp.arange(targets.shape[0], dtype=jnp.int32)
        return jnp.sum(jnp.where(hit, at[None, :] + 1, 0), axis=1) - 1

    root_table = picked(route_root)
    slots = picked(route_mid)
    mid_table = ((me - slots // CAP) % FRONTS) * CAP + slots % CAP

    own = jnp.concatenate([route_root, route_mid])
    every = jnp.stack([shifted(own, d) for d in range(FRONTS)])
    roots, mids = every[:, : route_root.shape[0]], every[:, route_root.shape[0] :]
    counts = jnp.sum((roots[:, None, :] == sources[None, :, None]).astype(jnp.int32), axis=-1)
    live_mid = (places[None, :] < counts[:, :1]).astype(jnp.int32).reshape(-1)
    order = (sources[None, :] == shifts[:, None]).astype(jnp.int32)
    by_front = jnp.sum(order[:, :, None] * counts[None, :, :], axis=1)
    flags = (places[None, None, :] < by_front.T[:, :, None]).astype(jnp.int32).reshape(FRONTS, -1)
    hit = (mids == me) & (flags > 0)
    mine = hit[:, None, :] & (ranks(mids)[:, None, :] == places[None, :, None])
    live_leaf = jnp.sum(mine.astype(jnp.int32), axis=-1).reshape(-1)
    return sources, root_table, mid_table, live_mid, live_leaf


def front_level(panels, refl, triangle, sources):
    partial = front_partial(panels, refl, sources)
    arrived = all_to_all(partial.reshape(32, COLS // 32, REFL), ROWS)
    return all_to_all(front_share(arrived, triangle), ROWS).reshape(COLS, REFL)


def per_device(
    panel_g, refl_root, refl_mid, refl_leaf, tri_root, tri_mid, tri_leaf, route_root, route_mid
):
    panel = panel_g.reshape(-1, COLS)
    y_root, y_mid, y_leaf = (y.reshape(-1, REFL) for y in (refl_root, refl_mid, refl_leaf))

    partial = root_partial(panel, y_root)
    arrived = all_to_all(partial.reshape(128, 8, 128), ALL)
    coeffs = all_to_all(root_share(arrived, tri_root), ALL).reshape(COLS * 4, 128)
    sources, root_table, mid_table, live_mid, live_leaf = tables(
        route_root.reshape(-1), route_mid.reshape(-1)
    )
    panels = exchange(root_apply(coeffs, panel, y_root, root_table))

    coeffs = front_level(panels, y_mid, tri_mid[0], sources)
    panels = exchange(front_apply(coeffs, panels, y_mid, sources, live_mid, mid_table))

    coeffs = front_level(panels, y_leaf, tri_leaf[0], sources)
    out = leaf_apply(coeffs, panels, y_leaf, sources, live_leaf)
    return out.reshape(refl_leaf.shape[:3] + (COLS,))


def solution(mesh):
    finer = Mesh(
        mesh.devices.reshape(mesh.shape["front"], 4, 4, 2), ("front", "rows_0", "rows_1", "rows_2")
    )
    rows = P("front", ROWS, None, None)
    placed = (
        rows,
        rows,
        rows,
        rows,
        P(),
        P("front", None, None),
        P("front", None, None),
        P("front", ROWS, None),
        P("front", ROWS, None),
    )
    return jax.shard_map(
        per_device,
        mesh=finer,
        in_specs=placed,
        out_specs=rows,
        check_vma=False,
    )
```

```python
import jax
import jax.numpy as jnp
from jax import lax
from jax.experimental import pallas as pl
from jax.experimental.pallas import tpu as pltpu
from jax.sharding import Mesh
from jax.sharding import PartitionSpec as P


BLOCK = 128
FRONTS = 4
CAP = 8
COLS = 256
REFL = 512
CHUNK = CAP * BLOCK
TILE = 512
ROWS = ("rows_0", "rows_1", "rows_2")
ALL = ("front",) + ROWS
F32 = jnp.float32
BF16 = jnp.bfloat16


def row_sums(panel, refl):
    return lax.dot_general(panel, refl, (((0,), (0,)), ((), ())), preferred_element_type=F32)


def times_coeffs(refl, coeffs_t):
    return lax.dot_general(refl, coeffs_t, (((1,), (1,)), ((), ())), preferred_element_type=F32)


VMEM = pl.BlockSpec(memory_space=pltpu.VMEM)
SMEM = pl.BlockSpec(memory_space=pltpu.SMEM)
HBM = pl.BlockSpec(memory_space=pltpu.MemorySpace.HBM)
DMA = pltpu.SemaphoreType.DMA


def local_call(kernel, outs, held=(), numbers=(), far=(), scratch=()):
    held = [pltpu.with_memory_space_constraint(a, pltpu.VMEM) for a in held]
    far = [pltpu.with_memory_space_constraint(a, pltpu.MemorySpace.HBM) for a in far]
    return pl.pallas_call(
        kernel,
        in_specs=[SMEM] * len(numbers) + [VMEM] * len(held) + [HBM] * len(far),
        out_specs=[spec for spec, _ in outs],
        out_shape=[shape for _, shape in outs],
        scratch_shapes=list(scratch),
        compiler_params=pltpu.CompilerParams(vmem_limit_bytes=12 << 20),
    )(*numbers, *held, *far)


def in_vmem(shape, dtype=BF16):
    return VMEM, pltpu.VMEM(shape, dtype)


def in_smem(count):
    return SMEM, jax.ShapeDtypeStruct((count,), jnp.int32)


def rows_at(block, count=1):
    return pl.ds(pl.multiple_of(block * BLOCK, BLOCK), count * BLOCK)


def root_partial(panel, refl, sources, route):
    rows = panel.shape[0]
    steps = rows // TILE

    def kernel(s_ref, r_ref, g_far, y_far, out_ref, g_ref, y_ref, s_out, r_out, tall_ref, acc_ref, sems):
        def copies(i):
            at = pl.ds(i * TILE, TILE)
            return [
                pltpu.make_async_copy(far.at[at], near.at[at], sems.at[k, i])
                for k, (far, near) in enumerate(((y_far, y_ref), (g_far, g_ref)))
            ]

        for i in range(steps):
            for copy in copies(i):
                copy.start()
        for taken, given in ((s_ref, s_out), (r_ref, r_out)):
            for i in range(taken.shape[0]):
                given[i] = taken[i]
        for i in range(steps):
            for copy in copies(i):
                copy.wait()
            at = slice(i * TILE, (i + 1) * TILE)
            part = row_sums(g_ref[at, :], y_ref[at, :])
            acc_ref[...] = part if i == 0 else acc_ref[...] + part
        for j in range(4):
            tall_ref[pl.ds(j, COLS, stride=4), :] = acc_ref[:, 128 * j : 128 * (j + 1)]
        out_ref[...] = tall_ref[...].astype(BF16)

    return local_call(
        kernel,
        [in_vmem((COLS * 4, 128)), in_vmem((rows, COLS)), in_vmem((rows, REFL))]
        + [in_smem(FRONTS), in_smem(route.shape[0])],
        numbers=[sources, route],
        far=[panel, refl],
        scratch=[pltpu.VMEM((COLS * 4, 128), F32), pltpu.VMEM((COLS, REFL), F32), DMA((2, steps))],
    )


def staged(triangle, refl, after):
    def kernel(after_ref, t_far, y_far, y_ref, high_ref, low_ref, t_ref, sems):
        triangle_copy = pltpu.make_async_copy(t_far, t_ref, sems.at[0])
        refl_copy = pltpu.make_async_copy(y_far, y_ref, sems.at[1])
        triangle_copy.start()
        refl_copy.start()
        triangle_copy.wait()
        high, low = split_bf16(t_ref[...])
        high_ref[...] = high
        low_ref[...] = low
        refl_copy.wait()

    return local_call(
        kernel,
        [in_vmem(refl.shape)] + [in_vmem((REFL, REFL))] * 2,
        numbers=[after],
        far=[triangle, refl],
        scratch=[pltpu.VMEM((REFL, REFL), F32), DMA((2,))],
    )


def front_partial(panels, refl, sources):
    def kernel(s_ref, g0, g1, g2, g3, y_ref, out_ref, acc_ref):
        for d, g_ref in enumerate((g0, g1, g2, g3)):
            part = row_sums(g_ref[...], y_ref[rows_at(s_ref[d] * CAP, CAP), :])
            acc_ref[...] = part if d == 0 else acc_ref[...] + part
        out_ref[...] = acc_ref[...].astype(BF16)

    return local_call(
        kernel,
        [in_vmem((COLS, REFL))],
        [*panels, refl],
        [sources],
        scratch=[pltpu.VMEM((COLS, REFL), F32)],
    )[0]


def split_bf16(x):
    high = x.astype(BF16)
    return high, (x - high.astype(F32)).astype(BF16)


def fine_dot(a, b_high, b_low):
    a_high, a_low = split_bf16(a)
    dot = lambda u, v: jnp.dot(u, v, preferred_element_type=F32)
    return dot(a_high, b_high) + (dot(a_low, b_high) + dot(a_high, b_low))


def root_share(arrived, triangle):
    def kernel(x_ref, t_ref, out_ref):
        total = jnp.sum(x_ref[...].astype(F32), axis=0)
        rows = [jnp.concatenate([total[4 * c + j : 4 * c + j + 1] for j in range(4)], 1) for c in range(2)]
        both = jnp.concatenate(rows + [jnp.zeros((6, REFL), F32)], axis=0)
        coeffs = fine_dot(both, *split_bf16(t_ref[...]))
        chunk = jnp.concatenate(
            [coeffs[c : c + 1, 128 * j : 128 * (j + 1)] for c in range(2) for j in range(4)], 0
        )
        out_ref[...] = jnp.broadcast_to(chunk.astype(BF16)[None], out_ref.shape)

    return local_call(kernel, [in_vmem(arrived.shape)], [arrived, triangle])[0]


def front_share(arrived, high, low):
    def kernel(x_ref, high_ref, low_ref, out_ref):
        total = jnp.sum(x_ref[...].astype(F32), axis=0)
        coeffs = fine_dot(total, high_ref[...], low_ref[...]).astype(BF16)
        out_ref[...] = jnp.broadcast_to(coeffs[None], out_ref.shape)

    return local_call(kernel, [in_vmem(arrived.shape)], [arrived, high, low])[0]


def scatter_blocks(table_ref, new_ref, out_refs, limit):
    for d in range(FRONTS):
        for p in range(CAP):
            at = table_ref[d * CAP + p]
            block = new_ref[rows_at(jnp.clip(at, 0, limit - 1)), :]
            out_refs[d][p * BLOCK : (p + 1) * BLOCK, :] = jnp.where(at >= 0, block, jnp.zeros_like(block))


CHUNKS = [in_vmem((CHUNK, COLS))] * FRONTS


def place_blocks(source_ref, route_ref, first, count, seen_ref, table_ref, number):
    mine = source_ref[0]
    for goal in range(FRONTS):
        seen_ref[goal] = 0

    def body(i, _):
        goal = route_ref[first + i]
        shift = jnp.bitwise_and(goal - mine, FRONTS - 1)
        table_ref[shift * CAP + seen_ref[goal]] = number(i)
        seen_ref[goal] = seen_ref[goal] + 1
        return 0

    lax.fori_loop(0, count, body, 0)


def root_apply(coeffs, panel, refl, sources, route):
    blocks = panel.shape[0] // BLOCK
    count = route.shape[0]

    def kernel(
        s_ref, r_ref, c_ref, g_ref, y_ref, o0, o1, o2, o3, same_ref, tall_ref, ct_ref, new_ref, seen_ref, t_ref
    ):
        for i in range(FRONTS * CAP):
            t_ref[i] = -1
        for i in range(count):
            same_ref[i] = r_ref[i]
        place_blocks(s_ref, r_ref, 0, blocks, seen_ref, t_ref, lambda i: i)
        tall_ref[...] = c_ref[...].astype(F32)
        for j in range(4):
            ct_ref[:, 128 * j : 128 * (j + 1)] = tall_ref[pl.ds(j, COLS, stride=4), :].astype(BF16)
        for i in range(blocks * BLOCK // TILE):
            at = slice(i * TILE, (i + 1) * TILE)
            new = g_ref[at, :].astype(F32) - times_coeffs(y_ref[at, :], ct_ref[...])
            new_ref[at, :] = new.astype(BF16)
        scatter_blocks(t_ref, new_ref, (o0, o1, o2, o3), blocks)

    return local_call(
        kernel,
        CHUNKS + [in_smem(count)],
        [coeffs, panel, refl],
        [sources, route],
        scratch=[
            pltpu.VMEM((COLS * 4, 128), F32),
            pltpu.VMEM((COLS, REFL), BF16),
            pltpu.VMEM(panel.shape, BF16),
            pltpu.SMEM((FRONTS,), jnp.int32),
            pltpu.SMEM((FRONTS * CAP,), jnp.int32),
        ],
    )


def updated(source_ref, live_ref, c_ref, g_refs, y_ref, write, after=lambda d: None):
    per = TILE // BLOCK
    for d in range(FRONTS):
        for i in range(CAP // per):
            first = source_ref[d] * CAP + i * per
            update = times_coeffs(y_ref[rows_at(first, per), :], c_ref[...])
            for b in range(per):
                place = i * per + b
                live = live_ref[d * CAP + place]
                old = g_refs[d][place * BLOCK : (place + 1) * BLOCK, :]
                new = old.astype(F32) - update[b * BLOCK : (b + 1) * BLOCK, :]
                write(d * CAP + place, jnp.where(live > 0, new, 0.0).astype(BF16))
        after(d)


def front_apply(coeffs, panels, refl, sources, live, table):
    def kernel(s_ref, l_ref, t_ref, c_ref, g0, g1, g2, g3, y_ref, o0, o1, o2, o3, new_ref):
        def write(place, value):
            new_ref[place * BLOCK : (place + 1) * BLOCK, :] = value

        updated(s_ref, l_ref, c_ref, (g0, g1, g2, g3), y_ref, write)
        scatter_blocks(t_ref, new_ref, (o0, o1, o2, o3), FRONTS * CAP)

    scratch = [pltpu.VMEM((FRONTS * CHUNK, COLS), BF16)]
    return local_call(
        kernel, CHUNKS, [coeffs, *panels, refl], [sources, live, table], scratch=scratch
    )


def leaf_apply(coeffs, panels, refl, sources, live):
    def kernel(s_ref, l_ref, c_ref, g0, g1, g2, g3, y_ref, out_far, new_ref, sems):
        def write(place, value):
            new_ref[place * BLOCK : (place + 1) * BLOCK, :] = value

        def leave(d):
            return pltpu.make_async_copy(
                new_ref.at[pl.ds(d * CHUNK, CHUNK)],
                out_far.at[rows_at(s_ref[d] * CAP, CAP)],
                sems.at[d],
            )

        updated(s_ref, l_ref, c_ref, (g0, g1, g2, g3), y_ref, write, lambda d: leave(d).start())
        for d in range(FRONTS):
            leave(d).wait()

    return local_call(
        kernel,
        [(HBM, jax.ShapeDtypeStruct((FRONTS * CHUNK, COLS), BF16))],
        [coeffs, *panels, refl],
        [sources, live],
        scratch=[pltpu.VMEM((FRONTS * CHUNK, COLS), BF16), DMA((FRONTS,))],
    )[0]


def shifted(x, d):
    return x if d == 0 else lax.ppermute(x, "front", [(i, (i + d) % FRONTS) for i in range(FRONTS)])


def exchange(outgoing):
    arrived = {d: shifted(outgoing[d], d) for d in (2, 1, 3, 0)}
    return [arrived[d] for d in range(FRONTS)]


def all_to_all(x, axes):
    return lax.all_to_all(x, axes, 0, 0, tiled=True)


def tables(sources, routes, blocks):
    slots = FRONTS * CAP

    def kernel(s_ref, r0, r1, r2, r3, mid_ref, live_mid_ref, live_leaf_ref, count_ref, seen_ref):
        mine = s_ref[0]
        every = (r0, r1, r2, r3)
        back = lambda front: jnp.bitwise_and(mine - front, FRONTS - 1)
        place_blocks(
            s_ref, r0, blocks, slots, seen_ref, mid_ref, lambda i: back(i // CAP) * CAP + i % CAP
        )
        for i in range(FRONTS * FRONTS):
            count_ref[i] = 0
        for d in range(FRONTS):

            def count(i, _, d=d):
                at = s_ref[d] * FRONTS + every[d][i]
                count_ref[at] = count_ref[at] + 1
                return 0

            lax.fori_loop(0, blocks, count, 0)
        for d in range(FRONTS):
            held = count_ref[s_ref[d] * FRONTS + mine]
            for p in range(CAP):
                live_mid_ref[d * CAP + p] = (p < held).astype(jnp.int32)

            def carry(i, seen, d=d):
                here = every[d][blocks + i] == mine
                sent = count_ref[(i // CAP) * FRONTS + s_ref[d]]

                @pl.when(here)
                def _():
                    live_leaf_ref[d * CAP + seen] = (i % CAP < sent).astype(jnp.int32)

                return seen + here.astype(jnp.int32)

            lax.fori_loop(0, slots, carry, jnp.int32(0))

    return local_call(
        kernel,
        [in_smem(slots)] * 3,
        numbers=[sources, *routes],
        scratch=[pltpu.SMEM((FRONTS * FRONTS,), jnp.int32), pltpu.SMEM((FRONTS,), jnp.int32)],
    )


def front_level(panels, staged_level, sources):
    refl, high, low = staged_level
    partial = front_partial(panels, refl, sources)
    arrived = all_to_all(partial.reshape(32, COLS // 32, REFL), ROWS)
    share = front_share(arrived, high, low)
    return all_to_all(share, ROWS).reshape(COLS, REFL)


def per_device(
    panel_g, refl_root, refl_mid, refl_leaf, tri_root, tri_mid, tri_leaf, route_root, route_mid
):
    panel = panel_g.reshape(-1, COLS)
    y_root, y_mid, y_leaf = (y.reshape(-1, REFL) for y in (refl_root, refl_mid, refl_leaf))
    sources = (lax.axis_index("front") - jnp.arange(FRONTS, dtype=jnp.int32)) % FRONTS
    own = jnp.concatenate([route_root.reshape(-1), route_mid.reshape(-1)])

    partial, panel, y_root, sources, own = root_partial(panel, y_root, sources, own)
    arrived = all_to_all(partial.reshape(128, 8, 128), ALL)
    share = root_share(arrived, tri_root)
    coeffs = all_to_all(share, ALL).reshape(COLS * 4, 128)
    *outgoing, own = root_apply(coeffs, panel, y_root, sources, own)
    panels = exchange(outgoing)

    routes = [shifted(own, d) for d in range(FRONTS)]
    middle = staged(tri_mid[0], y_mid, own)
    leaf = staged(tri_leaf[0], y_leaf, own)
    mid_table, live_mid, live_leaf = tables(sources, routes, route_root.size)

    coeffs = front_level(panels, middle, sources)
    outgoing = front_apply(coeffs, panels, middle[0], sources, live_mid, mid_table)
    panels = exchange(outgoing)

    coeffs = front_level(panels, leaf, sources)
    out = leaf_apply(coeffs, panels, leaf[0], sources, live_leaf)
    return out.reshape(refl_leaf.shape[:3] + (COLS,))


def solution(mesh):
    finer = Mesh(
        mesh.devices.reshape(mesh.shape["front"], 4, 4, 2), ("front", "rows_0", "rows_1", "rows_2")
    )
    rows = P("front", ROWS, None, None)
    placed = (
        rows,
        rows,
        rows,
        rows,
        P(),
        P("front", None, None),
        P("front", None, None),
        P("front", ROWS, None),
        P("front", ROWS, None),
    )
    return jax.shard_map(
        per_device,
        mesh=finer,
        in_specs=placed,
        out_specs=rows,
        check_vma=False,
    )
```

```python
import jax
import jax.numpy as jnp
from jax import lax
from jax.experimental import pallas as pl
from jax.experimental.pallas import tpu as pltpu
from jax.sharding import Mesh
from jax.sharding import PartitionSpec as P

BLOCK = 128
FRONTS = 4
CAP = 8
COLS = 256
REFL = 512
CHUNK = CAP * BLOCK
FLAGS = 16
TILE = 512
ROWS = ("rows_0", "rows_1", "rows_2")
ALL = ("front",) + ROWS
F32 = jnp.float32
BF16 = jnp.bfloat16


def row_sums(panel, refl):
    return lax.dot_general(panel, refl, (((0,), (0,)), ((), ())), preferred_element_type=F32)


def times_coeffs(refl, coeffs_t):
    return lax.dot_general(refl, coeffs_t, (((1,), (1,)), ((), ())), preferred_element_type=F32)


VMEM = pl.BlockSpec(memory_space=pltpu.VMEM)
SMEM = pl.BlockSpec(memory_space=pltpu.SMEM)
HBM = pl.BlockSpec(memory_space=pltpu.MemorySpace.HBM)
DMA = pltpu.SemaphoreType.DMA


def local_call(kernel, name, outs, held=(), numbers=(), far=(), scratch=()):
    held = [pltpu.with_memory_space_constraint(a, pltpu.VMEM) for a in held]
    far = [pltpu.with_memory_space_constraint(a, pltpu.MemorySpace.HBM) for a in far]
    with jax.named_scope(name):
        return pl.pallas_call(
            kernel,
            in_specs=[SMEM] * len(numbers) + [VMEM] * len(held) + [HBM] * len(far),
            out_specs=[spec for spec, _ in outs],
            out_shape=[shape for _, shape in outs],
            scratch_shapes=list(scratch),
            compiler_params=pltpu.CompilerParams(vmem_limit_bytes=12 << 20),
            name=name,
        )(*numbers, *held, *far)


def in_vmem(shape, dtype=BF16):
    return VMEM, pltpu.VMEM(shape, dtype)


def in_smem(count):
    return SMEM, jax.ShapeDtypeStruct((count,), jnp.int32)


def rows_at(block, count=1):
    return pl.ds(pl.multiple_of(block * BLOCK, BLOCK), count * BLOCK)


def root_partial(panel, refl, route_root, route_mid):
    rows = panel.shape[0]
    steps = rows // TILE
    slots = FRONTS * CAP

    def place_blocks(route_ref, table_ref, seen_ref):
        for goal in range(FRONTS):
            seen_ref[goal] = 0

        def body(i, _):
            goal = route_ref[i]
            table_ref[goal * CAP + seen_ref[goal]] = i
            seen_ref[goal] = seen_ref[goal] + 1
            return 0

        lax.fori_loop(0, route_ref.shape[0], body, 0)

    def kernel(
        g_far, y_far, r0_far, r1_far, out_ref, g_ref, y_ref, t0_ref, t1_ref, tall_ref, acc_ref, seen_ref, r0_ref, r1_ref, sems, route_sems
    ):
        routes = [
            pltpu.make_async_copy(r0_far, r0_ref, route_sems.at[0]),
            pltpu.make_async_copy(r1_far, r1_ref, route_sems.at[1]),
        ]
        for copy in routes:
            copy.start()

        def copies(i):
            at = pl.ds(i * TILE, TILE)
            return [
                pltpu.make_async_copy(far.at[at], near.at[at], sems.at[k, i])
                for k, (far, near) in enumerate(((y_far, y_ref), (g_far, g_ref)))
            ]

        for i in range(steps):
            for copy in copies(i):
                copy.start()
        for i in range(slots):
            t0_ref[i] = -1
        for copy in routes:
            copy.wait()
        place_blocks(r0_ref, t0_ref, seen_ref)
        place_blocks(r1_ref, t1_ref, seen_ref)
        for i in range(steps):
            for copy in copies(i):
                copy.wait()
            at = slice(i * TILE, (i + 1) * TILE)
            part = row_sums(g_ref[at, :], y_ref[at, :])
            acc_ref[...] = part if i == 0 else acc_ref[...] + part
        for j in range(4):
            tall_ref[pl.ds(j, COLS, stride=4), :] = acc_ref[:, 128 * j : 128 * (j + 1)]
        out_ref[...] = tall_ref[...].astype(BF16)

    return local_call(
        kernel,
        "root_partial",
        [in_vmem((COLS * 4, 128)), in_vmem((rows, COLS)), in_vmem((rows, REFL))]
        + [in_smem(slots), in_smem(slots)],
        far=[panel, refl, route_root, route_mid],
        scratch=[
            pltpu.VMEM((COLS * 4, 128), F32),
            pltpu.VMEM((COLS, REFL), F32),
            pltpu.SMEM((FRONTS,), jnp.int32),
            pltpu.SMEM(route_root.shape, jnp.int32),
            pltpu.SMEM(route_mid.shape, jnp.int32),
            DMA((2, steps)),
            DMA((2,)),
        ],
    )


def front_partial(chunks, refl):
    def kernel(g_ref, y_ref, out_ref, acc_ref):
        for f in range(FRONTS):
            part = row_sums(g_ref[f, :CHUNK, :], y_ref[f * CHUNK : (f + 1) * CHUNK, :])
            acc_ref[...] = part if f == 0 else acc_ref[...] + part
        out_ref[...] = acc_ref[...].astype(BF16)

    return local_call(
        kernel,
        "front_partial",
        [in_vmem((COLS, REFL))],
        [chunks, refl],
        scratch=[pltpu.VMEM((COLS, REFL), F32)],
    )[0]


def split_bf16(x):
    high = x.astype(BF16)
    return high, (x - high.astype(F32)).astype(BF16)


def fine_dot(a, b):
    a_high, a_low = split_bf16(a)
    b_high, b_low = split_bf16(b)
    dot = lambda u, v: jnp.dot(u, v, preferred_element_type=F32)
    return dot(a_high, b_high) + (dot(a_low, b_high) + dot(a_high, b_low))


def root_share(arrived, triangle):
    def kernel(x_ref, t_ref, out_ref):
        total = jnp.sum(x_ref[...].astype(F32), axis=0)
        rows = [jnp.concatenate([total[4 * c + j : 4 * c + j + 1] for j in range(4)], 1) for c in range(2)]
        both = jnp.concatenate(rows + [jnp.zeros((6, REFL), F32)], axis=0)
        coeffs = fine_dot(both, t_ref[...])
        chunk = jnp.concatenate(
            [coeffs[c : c + 1, 128 * j : 128 * (j + 1)] for c in range(2) for j in range(4)], 0
        )
        out_ref[...] = jnp.broadcast_to(chunk.astype(BF16)[None], out_ref.shape)

    return local_call(kernel, "root_share", [in_vmem(arrived.shape)], [arrived, triangle])[0]


def front_share(arrived, triangle):
    def kernel(x_ref, t_ref, out_ref):
        total = jnp.sum(x_ref[...].astype(F32), axis=0)
        coeffs = fine_dot(total, t_ref[...]).astype(BF16)
        out_ref[...] = jnp.broadcast_to(coeffs[None], out_ref.shape)

    return local_call(kernel, "front_share", [in_vmem(arrived.shape)], [arrived, triangle])[0]


LEAVING = in_vmem((FRONTS, CHUNK + FLAGS, COLS))


def root_apply(coeffs, panel, refl, table):
    blocks = panel.shape[0] // BLOCK

    def kernel(t_ref, c_ref, g_ref, y_ref, out_ref, tall_ref, ct_ref, new_ref):
        tall_ref[...] = c_ref[...].astype(F32)
        for j in range(4):
            ct_ref[:, 128 * j : 128 * (j + 1)] = tall_ref[pl.ds(j, COLS, stride=4), :].astype(BF16)
        for i in range(blocks * BLOCK // TILE):
            at = slice(i * TILE, (i + 1) * TILE)
            new = g_ref[at, :].astype(F32) - times_coeffs(y_ref[at, :], ct_ref[...])
            new_ref[at, :] = new.astype(BF16)
        row = lax.broadcasted_iota(jnp.int32, (FLAGS, COLS), 0)
        for f in range(FRONTS):
            flags = jnp.zeros((FLAGS, COLS), F32)
            for p in range(CAP):
                at = t_ref[f * CAP + p]
                block = new_ref[rows_at(jnp.maximum(at, 0)), :]
                out_ref[f, p * BLOCK : (p + 1) * BLOCK, :] = jnp.where(at >= 0, block, jnp.zeros_like(block))
                flags = jnp.where((row == p) & (at >= 0), 1.0, flags)
            out_ref[f, CHUNK:, :] = flags.astype(BF16)

    return local_call(
        kernel,
        "root_apply",
        [LEAVING],
        [coeffs, panel, refl],
        [table],
        scratch=[
            pltpu.VMEM((COLS * 4, 128), F32),
            pltpu.VMEM((COLS, REFL), BF16),
            pltpu.VMEM(panel.shape, BF16),
        ],
    )[0]


def updated(c_ref, g_ref, y_ref, write, after=lambda f, i: None):
    per = TILE // BLOCK
    for f in range(FRONTS):
        flags = g_ref[f, CHUNK:, :].astype(F32)
        for i in range(CAP // per):
            at = f * CHUNK + i * TILE
            update = times_coeffs(y_ref[at : at + TILE, :], c_ref[...])
            for b in range(per):
                p = i * per + b
                old = g_ref[f, p * BLOCK : (p + 1) * BLOCK, :].astype(F32)
                new = (old - update[b * BLOCK : (b + 1) * BLOCK, :]) * flags[p : p + 1, :]
                write(f * CAP + p, new.astype(BF16))
            after(f, i)


def front_apply(coeffs, chunks, refl, table):
    def kernel(t_ref, c_ref, g_ref, y_ref, out_ref, new_ref, flag_ref):
        def write(slot, value):
            new_ref[slot * BLOCK : (slot + 1) * BLOCK, :] = value

        updated(c_ref, g_ref, y_ref, write)
        for f in range(FRONTS):
            flag_ref[f * CAP : (f + 1) * CAP, :] = g_ref[f, CHUNK:, :].astype(F32)[:CAP]
        for f in range(FRONTS):
            rows = []
            for p in range(CAP):
                at = t_ref[f * CAP + p]
                out_ref[f, p * BLOCK : (p + 1) * BLOCK, :] = new_ref[rows_at(at), :]
                rows.append(flag_ref[pl.ds(at, 1), :])
            rows.append(jnp.zeros((FLAGS - CAP, COLS), F32))
            out_ref[f, CHUNK:, :] = jnp.concatenate(rows, axis=0).astype(BF16)

    return local_call(
        kernel,
        "front_apply",
        [LEAVING],
        [coeffs, chunks, refl],
        [table],
        scratch=[pltpu.VMEM((FRONTS * CHUNK, COLS), BF16), pltpu.VMEM((FRONTS * CAP, COLS), F32)],
    )[0]


def leaf_apply(coeffs, chunks, refl):
    per = CHUNK // TILE

    def kernel(c_ref, g_ref, y_ref, out_far, new_ref, sems):
        def write(slot, value):
            new_ref[slot * BLOCK : (slot + 1) * BLOCK, :] = value

        def leave(f, i):
            at = pl.ds((f * per + i) * TILE, TILE)
            return pltpu.make_async_copy(new_ref.at[at], out_far.at[at], sems.at[f * per + i])

        updated(c_ref, g_ref, y_ref, write, lambda f, i: leave(f, i).start())
        for f in range(FRONTS):
            for i in range(per):
                leave(f, i).wait()

    return local_call(
        kernel,
        "leaf_apply",
        [(HBM, jax.ShapeDtypeStruct((FRONTS * CHUNK, COLS), BF16))],
        [coeffs, chunks, refl],
        scratch=[pltpu.VMEM((FRONTS * CHUNK, COLS), BF16), DMA((FRONTS * per,))],
    )[0]


def all_to_all(x, axes):
    return lax.all_to_all(x, axes, 0, 0, tiled=True)


def front_level(chunks, refl, triangle):
    partial = front_partial(chunks, refl)
    arrived = all_to_all(partial.reshape(32, COLS // 32, REFL), ROWS)
    return all_to_all(front_share(arrived, triangle), ROWS).reshape(COLS, REFL)


def per_device(
    panel_g, refl_root, refl_mid, refl_leaf, tri_root, tri_mid, tri_leaf, route_root, route_mid
):
    panel = panel_g.reshape(-1, COLS)
    y_root, y_mid, y_leaf = (y.reshape(-1, REFL) for y in (refl_root, refl_mid, refl_leaf))

    partial, panel, y_root, root_table, mid_table = root_partial(
        panel, y_root, route_root.reshape(-1), route_mid.reshape(-1)
    )
    arrived = all_to_all(partial.reshape(128, 8, 128), ALL)
    coeffs = all_to_all(root_share(arrived, tri_root), ALL).reshape(COLS * 4, 128)
    chunks = all_to_all(root_apply(coeffs, panel, y_root, root_table), "front")

    coeffs = front_level(chunks, y_mid, tri_mid[0])
    chunks = all_to_all(front_apply(coeffs, chunks, y_mid, mid_table), "front")

    coeffs = front_level(chunks, y_leaf, tri_leaf[0])
    out = leaf_apply(coeffs, chunks, y_leaf)
    return out.reshape(refl_leaf.shape[:3] + (COLS,))


def solution(mesh):
    finer = Mesh(
        mesh.devices.reshape(mesh.shape["front"], 4, 4, 2), ("front", "rows_0", "rows_1", "rows_2")
    )
    rows = P("front", ROWS, None, None)
    placed = (
        rows,
        rows,
        rows,
        rows,
        P(),
        P("front", None, None),
        P("front", None, None),
        P("front", ROWS, None),
        P("front", ROWS, None),
    )
    return jax.shard_map(
        per_device,
        mesh=finer,
        in_specs=placed,
        out_specs=rows,
        check_vma=False,
    )
```

```python
import jax
import jax.numpy as jnp
from jax import lax
from jax.experimental import pallas as pl
from jax.experimental.pallas import tpu as pltpu
from jax.sharding import Mesh
from jax.sharding import PartitionSpec as P


BLOCK = 128
FRONTS = 4
CAP = 8
COLS = 256
REFL = 512
CHUNK = CAP * BLOCK
FLAGS = 16
TILE = 512
ROWS = ("rows_0", "rows_1", "rows_2")
ALL = ("front",) + ROWS
F32 = jnp.float32
BF16 = jnp.bfloat16


def row_sums(panel, refl):
    return lax.dot_general(panel, refl, (((0,), (0,)), ((), ())), preferred_element_type=F32)


def times_coeffs(refl, coeffs_t):
    return lax.dot_general(refl, coeffs_t, (((1,), (1,)), ((), ())), preferred_element_type=F32)


VMEM = pl.BlockSpec(memory_space=pltpu.VMEM)
SMEM = pl.BlockSpec(memory_space=pltpu.SMEM)
HBM = pl.BlockSpec(memory_space=pltpu.MemorySpace.HBM)
DMA = pltpu.SemaphoreType.DMA


def local_call(kernel, outs, held=(), numbers=(), far=(), scratch=()):
    held = [pltpu.with_memory_space_constraint(a, pltpu.VMEM) for a in held]
    far = [pltpu.with_memory_space_constraint(a, pltpu.MemorySpace.HBM) for a in far]
    return pl.pallas_call(
        kernel,
        in_specs=[SMEM] * len(numbers) + [VMEM] * len(held) + [HBM] * len(far),
        out_specs=[spec for spec, _ in outs],
        out_shape=[shape for _, shape in outs],
        scratch_shapes=list(scratch),
        compiler_params=pltpu.CompilerParams(vmem_limit_bytes=12 << 20),
    )(*numbers, *held, *far)


def in_vmem(shape, dtype=BF16):
    return VMEM, pltpu.VMEM(shape, dtype)


def in_smem(count):
    return SMEM, jax.ShapeDtypeStruct((count,), jnp.int32)


def rows_at(block, count=1):
    return pl.ds(pl.multiple_of(block * BLOCK, BLOCK), count * BLOCK)


def root_partial(panel, refl, route_root, route_mid):
    rows = panel.shape[0]
    steps = rows // TILE
    slots = FRONTS * CAP

    def place_blocks(route_ref, table_ref, seen_ref):
        for goal in range(FRONTS):
            seen_ref[goal] = 0

        def body(i, _):
            goal = route_ref[i]
            table_ref[goal * CAP + seen_ref[goal]] = i
            seen_ref[goal] = seen_ref[goal] + 1
            return 0

        lax.fori_loop(0, route_ref.shape[0], body, 0)

    def kernel(
        g_far, y_far, r0_far, r1_far, out_ref, g_ref, y_ref, t0_ref, t1_ref, tall_ref, acc_ref, seen_ref, r0_ref, r1_ref, sems, route_sems
    ):
        routes = [
            pltpu.make_async_copy(r0_far, r0_ref, route_sems.at[0]),
            pltpu.make_async_copy(r1_far, r1_ref, route_sems.at[1]),
        ]
        for copy in routes:
            copy.start()

        def copies(i):
            at = pl.ds(i * TILE, TILE)
            return [
                pltpu.make_async_copy(far.at[at], near.at[at], sems.at[k, i])
                for k, (far, near) in enumerate(((y_far, y_ref), (g_far, g_ref)))
            ]

        for i in range(steps):
            for copy in copies(i):
                copy.start()
        for i in range(slots):
            t0_ref[i] = -1
        for copy in routes:
            copy.wait()
        place_blocks(r0_ref, t0_ref, seen_ref)
        place_blocks(r1_ref, t1_ref, seen_ref)
        for i in range(steps):
            for copy in copies(i):
                copy.wait()
            at = slice(i * TILE, (i + 1) * TILE)
            part = row_sums(g_ref[at, :], y_ref[at, :])
            acc_ref[...] = part if i == 0 else acc_ref[...] + part
        for j in range(4):
            tall_ref[pl.ds(j, COLS, stride=4), :] = acc_ref[:, 128 * j : 128 * (j + 1)]
        out_ref[...] = tall_ref[...].astype(BF16)

    return local_call(
        kernel,
        [in_vmem((COLS * 4, 128)), in_vmem((rows, COLS)), in_vmem((rows, REFL))]
        + [in_smem(slots), in_smem(slots)],
        far=[panel, refl, route_root, route_mid],
        scratch=[
            pltpu.VMEM((COLS * 4, 128), F32),
            pltpu.VMEM((COLS, REFL), F32),
            pltpu.SMEM((FRONTS,), jnp.int32),
            pltpu.SMEM(route_root.shape, jnp.int32),
            pltpu.SMEM(route_mid.shape, jnp.int32),
            DMA((2, steps)),
            DMA((2,)),
        ],
    )


def ring_index(shift):
    return jnp.bitwise_and(lax.axis_index("front") + shift, FRONTS - 1)


def staged(refl, after):
    def kernel(after_ref, y_far, y_ref, sem):
        copy = pltpu.make_async_copy(y_far, y_ref, sem.at[0])
        copy.start()
        copy.wait()

    return local_call(
        kernel, [in_vmem(refl.shape)], numbers=[after], far=[refl], scratch=[DMA((1,))]
    )[0]


def front_partial(chunks, refl, before, last):
    shifts = list(chunks)
    ahead = [] if before is None else [before]

    def kernel(*refs):
        y_ref, out_ref, acc_ref = refs[-3], refs[-2], refs[-1]
        total = acc_ref if last else out_ref
        for k, d in enumerate(shifts):
            rows = y_ref[rows_at(ring_index(-d) * CAP, CAP), :]
            part = row_sums(refs[k][:CHUNK, :], rows)
            if k == 0 and before is not None:
                part = part + refs[len(shifts)][...]
            total[...] = part if k == 0 else total[...] + part
        if last:
            out_ref[...] = acc_ref[...].astype(BF16)

    return local_call(
        kernel,
        [in_vmem((COLS, REFL), BF16 if last else F32)],
        [*chunks.values(), *ahead, refl],
        scratch=[pltpu.VMEM((COLS, REFL), F32)],
    )[0]


def split_bf16(x):
    high = x.astype(BF16)
    return high, (x - high.astype(F32)).astype(BF16)


def fine_dot(a, b):
    a_high, a_low = split_bf16(a)
    b_high, b_low = split_bf16(b)
    dot = lambda u, v: jnp.dot(u, v, preferred_element_type=F32)
    return dot(a_high, b_high) + (dot(a_low, b_high) + dot(a_high, b_low))


def root_share(arrived, triangle):
    def kernel(x_ref, t_ref, out_ref):
        total = jnp.sum(x_ref[...].astype(F32), axis=0)
        rows = [jnp.concatenate([total[4 * c + j : 4 * c + j + 1] for j in range(4)], 1) for c in range(2)]
        both = jnp.concatenate(rows + [jnp.zeros((6, REFL), F32)], axis=0)
        coeffs = fine_dot(both, t_ref[...])
        chunk = jnp.concatenate(
            [coeffs[c : c + 1, 128 * j : 128 * (j + 1)] for c in range(2) for j in range(4)], 0
        )
        out_ref[...] = jnp.broadcast_to(chunk.astype(BF16)[None], out_ref.shape)

    return local_call(kernel, [in_vmem(arrived.shape)], [arrived, triangle])[0]


def front_share(arrived, triangle):
    def kernel(x_ref, t_ref, out_ref):
        total = jnp.sum(x_ref[...].astype(F32), axis=0)
        coeffs = fine_dot(total, t_ref[...]).astype(BF16)
        out_ref[...] = jnp.broadcast_to(coeffs[None], out_ref.shape)

    return local_call(kernel, [in_vmem(arrived.shape)], [arrived, triangle])[0]


LEAVING = in_vmem((CHUNK + FLAGS, COLS))
GATHERED = [pltpu.VMEM((CHUNK, REFL), BF16), pltpu.VMEM((CHUNK, COLS), F32)]


def leave(shift, table_ref, pick_panel, pick_flag, y_ref, ct_ref, out_ref, ys_ref, gs_ref):
    goal = ring_index(shift) * CAP
    flags = []
    for p in range(CAP):
        at = table_ref[goal + p]
        block = jnp.maximum(at, 0)
        here = slice(p * BLOCK, (p + 1) * BLOCK)
        ys_ref[here, :] = y_ref[rows_at(block), :]
        pick_panel(block, gs_ref, here)
        flags.append(pick_flag(at))
    for i in range(CHUNK // TILE):
        at = slice(i * TILE, (i + 1) * TILE)
        update = times_coeffs(ys_ref[at, :], ct_ref[...])
        for b in range(TILE // BLOCK):
            p = i * (TILE // BLOCK) + b
            here = slice(p * BLOCK, (p + 1) * BLOCK)
            new = (gs_ref[here, :] - update[b * BLOCK : (b + 1) * BLOCK, :]) * flags[p]
            out_ref[here, :] = new.astype(BF16)
    rows = flags + [jnp.zeros((FLAGS - CAP, COLS), F32)]
    out_ref[CHUNK:, :] = jnp.concatenate(rows, axis=0).astype(BF16)


def root_leave(shift, coeffs, panel, refl, table, first):
    def kernel(t_ref, c_ref, g_ref, y_ref, out_ref, *rest):
        if first:
            ct_ref, token_ref, tall_ref, ys_ref, gs_ref = rest
            token_ref[0] = 0
            tall_ref[...] = c_ref[...].astype(F32)
            for j in range(4):
                ct_ref[:, 128 * j : 128 * (j + 1)] = tall_ref[pl.ds(j, COLS, stride=4), :].astype(BF16)
        else:
            ct_ref, (ys_ref, gs_ref) = c_ref, rest

        def pick_panel(block, to_ref, here):
            to_ref[here, :] = g_ref[rows_at(block), :].astype(F32)

        def pick_flag(at):
            return jnp.broadcast_to(jnp.where(at >= 0, 1.0, 0.0).astype(F32), (1, COLS))

        leave(shift, t_ref, pick_panel, pick_flag, y_ref, ct_ref, out_ref, ys_ref, gs_ref)

    return local_call(
        kernel,
        [LEAVING] + ([in_vmem((COLS, REFL)), in_smem(1)] if first else []),
        [coeffs, panel, refl],
        [table],
        scratch=([pltpu.VMEM((COLS * 4, 128), F32)] if first else []) + GATHERED,
    )


def front_leave(shift, coeffs, chunks, refl, table, first):
    def kernel(t_ref, c_ref, g0, g1, g2, g3, y_ref, out_ref, *rest):
        *token, ys_ref, gs_ref, flag_ref = rest
        for token_ref in token:
            token_ref[0] = 0
        for d, g_ref in enumerate((g0, g1, g2, g3)):
            flag_ref[d * FLAGS : (d + 1) * FLAGS, :] = g_ref[CHUNK:, :].astype(F32)

        def chunk_of(block):
            return ring_index(-(block // CAP)), block % CAP

        def pick_panel(block, to_ref, here):
            chunk, place = chunk_of(block)
            for d, g_ref in enumerate((g0, g1, g2, g3)):

                @pl.when(chunk == d)
                def _():
                    to_ref[here, :] = g_ref[rows_at(place), :].astype(F32)

        def pick_flag(at):
            chunk, place = chunk_of(at)
            return flag_ref[pl.ds(chunk * FLAGS + place, 1), :]

        leave(shift, t_ref, pick_panel, pick_flag, y_ref, c_ref, out_ref, ys_ref, gs_ref)

    return local_call(
        kernel,
        [LEAVING] + ([in_smem(1)] if first else []),
        [coeffs, *chunks, refl],
        [table],
        scratch=GATHERED + [pltpu.VMEM((FRONTS * FLAGS, COLS), F32)],
    )


def leaf_apply(coeffs, chunks, refl):
    per = CHUNK // TILE
    blocks = TILE // BLOCK

    def kernel(c_ref, g0, g1, g2, g3, y_ref, out_far, new_ref, sems):
        def leaving(d, i):
            return pltpu.make_async_copy(
                new_ref.at[pl.ds((d * per + i) * TILE, TILE)],
                out_far.at[rows_at(ring_index(-d) * CAP + i * blocks, blocks)],
                sems.at[d * per + i],
            )

        for d, g_ref in enumerate((g0, g1, g2, g3)):
            flags = g_ref[CHUNK:, :].astype(F32)
            for i in range(per):
                rows = rows_at(ring_index(-d) * CAP + i * blocks, blocks)
                update = times_coeffs(y_ref[rows, :], c_ref[...])
                for b in range(blocks):
                    p = i * blocks + b
                    old = g_ref[p * BLOCK : (p + 1) * BLOCK, :].astype(F32)
                    new = (old - update[b * BLOCK : (b + 1) * BLOCK, :]) * flags[p : p + 1, :]
                    at = d * CHUNK + p * BLOCK
                    new_ref[at : at + BLOCK, :] = new.astype(BF16)
                leaving(d, i).start()
        for d in range(FRONTS):
            for i in range(per):
                leaving(d, i).wait()

    return local_call(
        kernel,
        [(HBM, jax.ShapeDtypeStruct((FRONTS * CHUNK, COLS), BF16))],
        [coeffs, *chunks, refl],
        scratch=[pltpu.VMEM((FRONTS * CHUNK, COLS), BF16), DMA((FRONTS * per,))],
    )[0]


def all_to_all(x, axes):
    return lax.all_to_all(x, axes, 0, 0, tiled=True)


def shifted(x, d):
    return lax.ppermute(x, "front", [(i, (i + d) % FRONTS) for i in range(FRONTS)])


ORDER = (2, 1, 3)


def route(leaving):
    chunks = {}
    for d in ORDER + (0,):
        out = leaving(d)
        chunks[d] = shifted(out, d) if d else out
    return [chunks[d] for d in range(FRONTS)]


def front_level(chunks, refl, triangle):
    total = front_partial({0: chunks[0]}, refl, None, False)
    total = front_partial({1: chunks[1], 3: chunks[3]}, refl, total, False)
    partial = front_partial({2: chunks[2]}, refl, total, True)
    arrived = all_to_all(partial.reshape(32, COLS // 32, REFL), ROWS)
    return all_to_all(front_share(arrived, triangle), ROWS).reshape(COLS, REFL)


def per_device(
    panel_g, refl_root, refl_mid, refl_leaf, tri_root, tri_mid, tri_leaf, route_root, route_mid
):
    panel = panel_g.reshape(-1, COLS)
    y_root, y_mid, y_leaf = (y.reshape(-1, REFL) for y in (refl_root, refl_mid, refl_leaf))

    partial, panel, y_root, root_table, mid_table = root_partial(
        panel, y_root, route_root.reshape(-1), route_mid.reshape(-1)
    )
    arrived = all_to_all(partial.reshape(128, 8, 128), ALL)
    coeffs = all_to_all(root_share(arrived, tri_root), ALL).reshape(COLS * 4, 128)
    token = None

    def from_root(d):
        nonlocal coeffs, token
        out = root_leave(d, coeffs, panel, y_root, root_table, token is None)
        if token is None:
            _, coeffs, token = out
        return out[0]

    chunks = route(from_root)
    y_mid = staged(y_mid, token)
    coeffs = front_level(chunks, y_mid, tri_mid[0])
    arrived, token = chunks, None

    def from_middle(d):
        nonlocal token
        out = front_leave(d, coeffs, arrived, y_mid, mid_table, token is None)
        if token is None:
            token = out[1]
        return out[0]

    chunks = route(from_middle)
    y_leaf = staged(y_leaf, token)
    coeffs = front_level(chunks, y_leaf, tri_leaf[0])
    out = leaf_apply(coeffs, chunks, y_leaf)
    return out.reshape(refl_leaf.shape[:3] + (COLS,))


def solution(mesh):
    finer = Mesh(
        mesh.devices.reshape(mesh.shape["front"], 4, 4, 2), ("front", "rows_0", "rows_1", "rows_2")
    )
    rows = P("front", ROWS, None, None)
    placed = (
        rows,
        rows,
        rows,
        rows,
        P(),
        P("front", None, None),
        P("front", None, None),
        P("front", ROWS, None),
        P("front", ROWS, None),
    )
    return jax.shard_map(
        per_device,
        mesh=finer,
        in_specs=placed,
        out_specs=rows,
        check_vma=False,
    )
```

```python
import jax
import jax.numpy as jnp
from jax import lax
from jax.experimental import pallas as pl
from jax.experimental.pallas import tpu as pltpu
from jax.sharding import Mesh
from jax.sharding import PartitionSpec as P


BLOCK = 128
FRONTS = 4
CAP = 8
COLS = 256
REFL = 512
CHUNK = CAP * BLOCK
FLAGS = 16
TILE = 512
ROWS = ("rows_0", "rows_1", "rows_2")
ALL = ("front",) + ROWS
F32 = jnp.float32
BF16 = jnp.bfloat16


def row_sums(panel, refl):
    return lax.dot_general(panel, refl, (((0,), (0,)), ((), ())), preferred_element_type=F32)


def times_coeffs(refl, coeffs_t):
    return lax.dot_general(refl, coeffs_t, (((1,), (1,)), ((), ())), preferred_element_type=F32)


VMEM = pl.BlockSpec(memory_space=pltpu.VMEM)
SMEM = pl.BlockSpec(memory_space=pltpu.SMEM)
HBM = pl.BlockSpec(memory_space=pltpu.MemorySpace.HBM)
DMA = pltpu.SemaphoreType.DMA


def local_call(kernel, outs, held=(), numbers=(), far=(), scratch=()):
    held = [pltpu.with_memory_space_constraint(a, pltpu.VMEM) for a in held]
    far = [pltpu.with_memory_space_constraint(a, pltpu.MemorySpace.HBM) for a in far]
    return pl.pallas_call(
        kernel,
        in_specs=[SMEM] * len(numbers) + [VMEM] * len(held) + [HBM] * len(far),
        out_specs=[spec for spec, _ in outs],
        out_shape=[shape for _, shape in outs],
        scratch_shapes=list(scratch),
        compiler_params=pltpu.CompilerParams(vmem_limit_bytes=12 << 20),
    )(*numbers, *held, *far)


def in_vmem(shape, dtype=BF16):
    return VMEM, pltpu.VMEM(shape, dtype)


def in_smem(count):
    return SMEM, jax.ShapeDtypeStruct((count,), jnp.int32)


def rows_at(block, count=1):
    return pl.ds(pl.multiple_of(block * BLOCK, BLOCK), count * BLOCK)


def root_partial(panel, refl, route_root, route_mid):
    rows = panel.shape[0]
    steps = rows // TILE
    slots = FRONTS * CAP

    def place_blocks(route_ref, table_ref, seen_ref):
        for goal in range(FRONTS):
            seen_ref[goal] = 0

        def body(i, _):
            goal = route_ref[i]
            table_ref[goal * CAP + seen_ref[goal]] = i
            seen_ref[goal] = seen_ref[goal] + 1
            return 0

        lax.fori_loop(0, route_ref.shape[0], body, 0)

    def kernel(
        g_far, y_far, r0_far, r1_far, out_ref, g_ref, y_ref, t0_ref, t1_ref, tall_ref, acc_ref, seen_ref, r0_ref, r1_ref, sems, route_sems
    ):
        routes = [
            pltpu.make_async_copy(r0_far, r0_ref, route_sems.at[0]),
            pltpu.make_async_copy(r1_far, r1_ref, route_sems.at[1]),
        ]
        for copy in routes:
            copy.start()

        def copies(i):
            at = pl.ds(i * TILE, TILE)
            return [
                pltpu.make_async_copy(far.at[at], near.at[at], sems.at[k, i])
                for k, (far, near) in enumerate(((y_far, y_ref), (g_far, g_ref)))
            ]

        for i in range(steps):
            for copy in copies(i):
                copy.start()
        for i in range(slots):
            t0_ref[i] = -1
        for copy in routes:
            copy.wait()
        place_blocks(r0_ref, t0_ref, seen_ref)
        place_blocks(r1_ref, t1_ref, seen_ref)
        for i in range(steps):
            for copy in copies(i):
                copy.wait()
            at = slice(i * TILE, (i + 1) * TILE)
            part = row_sums(g_ref[at, :], y_ref[at, :])
            acc_ref[...] = part if i == 0 else acc_ref[...] + part
        for j in range(4):
            tall_ref[pl.ds(j, COLS, stride=4), :] = acc_ref[:, 128 * j : 128 * (j + 1)]
        out_ref[...] = tall_ref[...].astype(BF16)

    return local_call(
        kernel,
        [in_vmem((COLS * 4, 128)), in_vmem((rows, COLS)), in_vmem((rows, REFL))]
        + [in_smem(slots), in_smem(slots)],
        far=[panel, refl, route_root, route_mid],
        scratch=[
            pltpu.VMEM((COLS * 4, 128), F32),
            pltpu.VMEM((COLS, REFL), F32),
            pltpu.SMEM((FRONTS,), jnp.int32),
            pltpu.SMEM(route_root.shape, jnp.int32),
            pltpu.SMEM(route_mid.shape, jnp.int32),
            DMA((2, steps)),
            DMA((2,)),
        ],
    )


def ring_index(shift):
    return jnp.bitwise_and(lax.axis_index("front") + shift, FRONTS - 1)


def staged(refl, after):
    def kernel(after_ref, y_far, y_ref, sem):
        copy = pltpu.make_async_copy(y_far, y_ref, sem.at[0])
        copy.start()
        copy.wait()

    return local_call(
        kernel, [in_vmem(refl.shape)], numbers=[after], far=[refl], scratch=[DMA((1,))]
    )[0]


def front_partial(chunks, refl, before, last):
    shifts = list(chunks)
    ahead = [] if before is None else [before]

    def kernel(*refs):
        y_ref, out_ref, acc_ref = refs[-3], refs[-2], refs[-1]
        total = acc_ref if last else out_ref
        for k, d in enumerate(shifts):
            rows = y_ref[rows_at(ring_index(-d) * CAP, CAP), :]
            part = row_sums(refs[k][:CHUNK, :], rows)
            if k == 0 and before is not None:
                part = part + refs[len(shifts)][...]
            total[...] = part if k == 0 else total[...] + part
        if last:
            out_ref[...] = acc_ref[...].astype(BF16)

    return local_call(
        kernel,
        [in_vmem((COLS, REFL), BF16 if last else F32)],
        [*chunks.values(), *ahead, refl],
        scratch=[pltpu.VMEM((COLS, REFL), F32)],
    )[0]


def split_bf16(x):
    high = x.astype(BF16)
    return high, (x - high.astype(F32)).astype(BF16)


def fine_dot(a, b):
    a_high, a_low = split_bf16(a)
    b_high, b_low = split_bf16(b)
    dot = lambda u, v: jnp.dot(u, v, preferred_element_type=F32)
    return dot(a_high, b_high) + (dot(a_low, b_high) + dot(a_high, b_low))


def root_share(arrived, triangle):
    def kernel(x_ref, t_ref, out_ref):
        total = jnp.sum(x_ref[...].astype(F32), axis=0)
        rows = [jnp.concatenate([total[4 * c + j : 4 * c + j + 1] for j in range(4)], 1) for c in range(2)]
        both = jnp.concatenate(rows + [jnp.zeros((6, REFL), F32)], axis=0)
        coeffs = fine_dot(both, t_ref[...])
        chunk = jnp.concatenate(
            [coeffs[c : c + 1, 128 * j : 128 * (j + 1)] for c in range(2) for j in range(4)], 0
        )
        out_ref[...] = jnp.broadcast_to(chunk.astype(BF16)[None], out_ref.shape)

    return local_call(kernel, [in_vmem(arrived.shape)], [arrived, triangle])[0]


def front_share(arrived, triangle):
    def kernel(x_ref, t_ref, out_ref):
        total = jnp.sum(x_ref[...].astype(F32), axis=0)
        coeffs = fine_dot(total, t_ref[...]).astype(BF16)
        out_ref[...] = jnp.broadcast_to(coeffs[None], out_ref.shape)

    return local_call(kernel, [in_vmem(arrived.shape)], [arrived, triangle])[0]


LEAVING = in_vmem((CHUNK + FLAGS, COLS))
GATHERED = [pltpu.VMEM((CHUNK, REFL), BF16), pltpu.VMEM((CHUNK, COLS), F32)]


def leave(shift, table_ref, pick_panel, pick_flag, y_ref, ct_ref, out_ref, ys_ref, gs_ref):
    goal = ring_index(shift) * CAP
    flags = []
    for p in range(CAP):
        at = table_ref[goal + p]
        block = jnp.maximum(at, 0)
        here = slice(p * BLOCK, (p + 1) * BLOCK)
        ys_ref[here, :] = y_ref[rows_at(block), :]
        pick_panel(block, gs_ref, here)
        flags.append(pick_flag(at))
    for i in range(CHUNK // TILE):
        at = slice(i * TILE, (i + 1) * TILE)
        update = times_coeffs(ys_ref[at, :], ct_ref[...])
        for b in range(TILE // BLOCK):
            p = i * (TILE // BLOCK) + b
            here = slice(p * BLOCK, (p + 1) * BLOCK)
            new = (gs_ref[here, :] - update[b * BLOCK : (b + 1) * BLOCK, :]) * flags[p]
            out_ref[here, :] = new.astype(BF16)
    rows = flags + [jnp.zeros((FLAGS - CAP, COLS), F32)]
    out_ref[CHUNK:, :] = jnp.concatenate(rows, axis=0).astype(BF16)


def root_leave(shift, coeffs, panel, refl, table, first):
    def kernel(t_ref, c_ref, g_ref, y_ref, out_ref, *rest):
        if first:
            ct_ref, token_ref, tall_ref, ys_ref, gs_ref = rest
            token_ref[0] = 0
            tall_ref[...] = c_ref[...].astype(F32)
            for j in range(4):
                ct_ref[:, 128 * j : 128 * (j + 1)] = tall_ref[pl.ds(j, COLS, stride=4), :].astype(BF16)
        else:
            ct_ref, (ys_ref, gs_ref) = c_ref, rest

        def pick_panel(block, to_ref, here):
            to_ref[here, :] = g_ref[rows_at(block), :].astype(F32)

        def pick_flag(at):
            return jnp.broadcast_to(jnp.where(at >= 0, 1.0, 0.0).astype(F32), (1, COLS))

        leave(shift, t_ref, pick_panel, pick_flag, y_ref, ct_ref, out_ref, ys_ref, gs_ref)

    return local_call(
        kernel,
        [LEAVING] + ([in_vmem((COLS, REFL)), in_smem(1)] if first else []),
        [coeffs, panel, refl],
        [table],
        scratch=([pltpu.VMEM((COLS * 4, 128), F32)] if first else []) + GATHERED,
    )


def front_leave(shift, coeffs, chunks, refl, table, first):
    def kernel(t_ref, c_ref, g0, g1, g2, g3, y_ref, out_ref, *rest):
        *token, ys_ref, gs_ref, flag_ref = rest
        for token_ref in token:
            token_ref[0] = 0
        for d, g_ref in enumerate((g0, g1, g2, g3)):
            flag_ref[d * FLAGS : (d + 1) * FLAGS, :] = g_ref[CHUNK:, :].astype(F32)

        def chunk_of(block):
            return ring_index(-(block // CAP)), block % CAP

        def pick_panel(block, to_ref, here):
            chunk, place = chunk_of(block)
            for d, g_ref in enumerate((g0, g1, g2, g3)):

                @pl.when(chunk == d)
                def _():
                    to_ref[here, :] = g_ref[rows_at(place), :].astype(F32)

        def pick_flag(at):
            chunk, place = chunk_of(at)
            return flag_ref[pl.ds(chunk * FLAGS + place, 1), :]

        leave(shift, t_ref, pick_panel, pick_flag, y_ref, c_ref, out_ref, ys_ref, gs_ref)

    return local_call(
        kernel,
        [LEAVING] + ([in_smem(1)] if first else []),
        [coeffs, *chunks, refl],
        [table],
        scratch=GATHERED + [pltpu.VMEM((FRONTS * FLAGS, COLS), F32)],
    )


def leaf_apply(coeffs, chunks, refl):
    per = CHUNK // TILE
    blocks = TILE // BLOCK

    def kernel(c_ref, g0, g1, g2, g3, y_ref, out_far, new_ref, sems):
        def leaving(d, i):
            return pltpu.make_async_copy(
                new_ref.at[pl.ds((d * per + i) * TILE, TILE)],
                out_far.at[rows_at(ring_index(-d) * CAP + i * blocks, blocks)],
                sems.at[d * per + i],
            )

        for d, g_ref in enumerate((g0, g1, g2, g3)):
            flags = g_ref[CHUNK:, :].astype(F32)
            for i in range(per):
                rows = rows_at(ring_index(-d) * CAP + i * blocks, blocks)
                update = times_coeffs(y_ref[rows, :], c_ref[...])
                for b in range(blocks):
                    p = i * blocks + b
                    old = g_ref[p * BLOCK : (p + 1) * BLOCK, :].astype(F32)
                    new = (old - update[b * BLOCK : (b + 1) * BLOCK, :]) * flags[p : p + 1, :]
                    at = d * CHUNK + p * BLOCK
                    new_ref[at : at + BLOCK, :] = new.astype(BF16)
                leaving(d, i).start()
        for d in range(FRONTS):
            for i in range(per):
                leaving(d, i).wait()

    return local_call(
        kernel,
        [(HBM, jax.ShapeDtypeStruct((FRONTS * CHUNK, COLS), BF16))],
        [coeffs, *chunks, refl],
        scratch=[pltpu.VMEM((FRONTS * CHUNK, COLS), BF16), DMA((FRONTS * per,))],
    )[0]


def all_to_all(x, axes):
    return lax.all_to_all(x, axes, 0, 0, tiled=True)


def shifted(x, d):
    return lax.ppermute(x, "front", [(i, (i + d) % FRONTS) for i in range(FRONTS)])


ORDER = (2, 1, 3)


def route(leaving):
    chunks = {}
    for d in ORDER + (0,):
        out = leaving(d)
        chunks[d] = shifted(out, d) if d else out
    return [chunks[d] for d in range(FRONTS)]


def front_level(chunks, refl, triangle):
    partial = None
    for d in (0,) + ORDER:
        partial = front_partial({d: chunks[d]}, refl, partial, d == ORDER[-1])
    arrived = all_to_all(partial.reshape(32, COLS // 32, REFL), ROWS)
    return all_to_all(front_share(arrived, triangle), ROWS).reshape(COLS, REFL)


def per_device(
    panel_g, refl_root, refl_mid, refl_leaf, tri_root, tri_mid, tri_leaf, route_root, route_mid
):
    panel = panel_g.reshape(-1, COLS)
    y_root, y_mid, y_leaf = (y.reshape(-1, REFL) for y in (refl_root, refl_mid, refl_leaf))

    partial, panel, y_root, root_table, mid_table = root_partial(
        panel, y_root, route_root.reshape(-1), route_mid.reshape(-1)
    )
    arrived = all_to_all(partial.reshape(128, 8, 128), ALL)
    coeffs = all_to_all(root_share(arrived, tri_root), ALL).reshape(COLS * 4, 128)
    token = None

    def from_root(d):
        nonlocal coeffs, token
        out = root_leave(d, coeffs, panel, y_root, root_table, token is None)
        if token is None:
            _, coeffs, token = out
        return out[0]

    chunks = route(from_root)
    y_mid = staged(y_mid, token)
    coeffs = front_level(chunks, y_mid, tri_mid[0])
    arrived, token = chunks, None

    def from_middle(d):
        nonlocal token
        out = front_leave(d, coeffs, arrived, y_mid, mid_table, token is None)
        if token is None:
            token = out[1]
        return out[0]

    chunks = route(from_middle)
    y_leaf = staged(y_leaf, token)
    coeffs = front_level(chunks, y_leaf, tri_leaf[0])
    out = leaf_apply(coeffs, chunks, y_leaf)
    return out.reshape(refl_leaf.shape[:3] + (COLS,))


def solution(mesh):
    finer = Mesh(
        mesh.devices.reshape(mesh.shape["front"], 4, 4, 2), ("front", "rows_0", "rows_1", "rows_2")
    )
    rows = P("front", ROWS, None, None)
    placed = (
        rows,
        rows,
        rows,
        rows,
        P(),
        P("front", None, None),
        P("front", None, None),
        P("front", ROWS, None),
        P("front", ROWS, None),
    )
    return jax.shard_map(
        per_device,
        mesh=finer,
        in_specs=placed,
        out_specs=rows,
        check_vma=False,
    )
```

```python
import jax
import jax.numpy as jnp
from jax import lax
from jax.experimental import pallas as pl
from jax.experimental.pallas import tpu as pltpu
from jax.sharding import Mesh
from jax.sharding import PartitionSpec as P


BLOCK = 128
FRONTS = 4
CAP = 8
COLS = 256
REFL = 512
CHUNK = CAP * BLOCK
FLAGS = 16
TILE = 512
ROWS = ("rows_0", "rows_1", "rows_2")
ALL = ("front",) + ROWS
F32 = jnp.float32
BF16 = jnp.bfloat16


def row_sums(panel, refl):
    return lax.dot_general(panel, refl, (((0,), (0,)), ((), ())), preferred_element_type=F32)


def times_coeffs(refl, coeffs_t):
    return lax.dot_general(refl, coeffs_t, (((1,), (1,)), ((), ())), preferred_element_type=F32)


VMEM = pl.BlockSpec(memory_space=pltpu.VMEM)
SMEM = pl.BlockSpec(memory_space=pltpu.SMEM)
HBM = pl.BlockSpec(memory_space=pltpu.MemorySpace.HBM)
DMA = pltpu.SemaphoreType.DMA


def local_call(kernel, outs, held=(), numbers=(), far=(), scratch=()):
    held = [pltpu.with_memory_space_constraint(a, pltpu.VMEM) for a in held]
    far = [pltpu.with_memory_space_constraint(a, pltpu.MemorySpace.HBM) for a in far]
    return pl.pallas_call(
        kernel,
        in_specs=[SMEM] * len(numbers) + [VMEM] * len(held) + [HBM] * len(far),
        out_specs=[spec for spec, _ in outs],
        out_shape=[shape for _, shape in outs],
        scratch_shapes=list(scratch),
        compiler_params=pltpu.CompilerParams(vmem_limit_bytes=12 << 20),
    )(*numbers, *held, *far)


def in_vmem(shape, dtype=BF16):
    return VMEM, pltpu.VMEM(shape, dtype)


def in_smem(count):
    return SMEM, jax.ShapeDtypeStruct((count,), jnp.int32)


def rows_at(block, count=1):
    return pl.ds(pl.multiple_of(block * BLOCK, BLOCK), count * BLOCK)


def root_partial(panel, refl, route_root, route_mid):
    rows = panel.shape[0]
    steps = rows // TILE
    slots = FRONTS * CAP

    def place_blocks(route_ref, table_ref, seen_ref):
        for goal in range(FRONTS):
            seen_ref[goal] = 0

        def body(i, _):
            goal = route_ref[i]
            table_ref[goal * CAP + seen_ref[goal]] = i
            seen_ref[goal] = seen_ref[goal] + 1
            return 0

        lax.fori_loop(0, route_ref.shape[0], body, 0)

    def kernel(
        g_far, y_far, r0_far, r1_far, out_ref, g_ref, y_ref, t0_ref, t1_ref, tall_ref, acc_ref, seen_ref, r0_ref, r1_ref, sems, route_sems
    ):
        routes = [
            pltpu.make_async_copy(r0_far, r0_ref, route_sems.at[0]),
            pltpu.make_async_copy(r1_far, r1_ref, route_sems.at[1]),
        ]
        for copy in routes:
            copy.start()

        def copies(i):
            at = pl.ds(i * TILE, TILE)
            return [
                pltpu.make_async_copy(far.at[at], near.at[at], sems.at[k, i])
                for k, (far, near) in enumerate(((y_far, y_ref), (g_far, g_ref)))
            ]

        for i in range(steps):
            for copy in copies(i):
                copy.start()
        for i in range(slots):
            t0_ref[i] = -1
        for copy in routes:
            copy.wait()
        place_blocks(r0_ref, t0_ref, seen_ref)
        place_blocks(r1_ref, t1_ref, seen_ref)
        for i in range(steps):
            for copy in copies(i):
                copy.wait()
            at = slice(i * TILE, (i + 1) * TILE)
            part = row_sums(g_ref[at, :], y_ref[at, :])
            acc_ref[...] = part if i == 0 else acc_ref[...] + part
        for j in range(4):
            tall_ref[pl.ds(j, COLS, stride=4), :] = acc_ref[:, 128 * j : 128 * (j + 1)]
        out_ref[...] = tall_ref[...].astype(BF16)

    return local_call(
        kernel,
        [in_vmem((COLS * 4, 128)), in_vmem((rows, COLS)), in_vmem((rows, REFL))]
        + [in_smem(slots), in_smem(slots)],
        far=[panel, refl, route_root, route_mid],
        scratch=[
            pltpu.VMEM((COLS * 4, 128), F32),
            pltpu.VMEM((COLS, REFL), F32),
            pltpu.SMEM((FRONTS,), jnp.int32),
            pltpu.SMEM(route_root.shape, jnp.int32),
            pltpu.SMEM(route_mid.shape, jnp.int32),
            DMA((2, steps)),
            DMA((2,)),
        ],
    )


def ring_index(shift):
    return jnp.bitwise_and(lax.axis_index("front") + shift, FRONTS - 1)


def staged(refl, triangle, after, table):
    ordered = table is not None
    slots = FRONTS * CAP

    def kernel(*refs):
        if ordered:
            _, table_ref, y_far, t_far, y_ref, high_ref, low_ref, order_ref, t_ref, sems, order_sems = refs
        else:
            _, y_far, t_far, y_ref, high_ref, low_ref, t_ref, sems = refs
        triangle_copy = pltpu.make_async_copy(t_far, t_ref, sems.at[0])
        refl_copy = pltpu.make_async_copy(y_far, y_ref, sems.at[1])
        triangle_copy.start()
        refl_copy.start()
        triangle_copy.wait()
        high, low = split_bf16(t_ref[...])
        high_ref[...] = high
        low_ref[...] = low
        if ordered:
            blocks = [
                pltpu.make_async_copy(
                    y_far.at[rows_at(table_ref[k])],
                    order_ref.at[pl.ds(k * BLOCK, BLOCK)],
                    order_sems.at[k],
                )
                for k in range(slots)
            ]
            for copy in blocks:
                copy.start()
            for copy in blocks:
                copy.wait()
        refl_copy.wait()

    return local_call(
        kernel,
        [in_vmem(refl.shape)] + [in_vmem((REFL, REFL))] * 2 + ([in_vmem(refl.shape)] if ordered else []),
        numbers=[after] + ([table] if ordered else []),
        far=[refl, triangle],
        scratch=[pltpu.VMEM((REFL, REFL), F32), DMA((2,))] + ([DMA((slots,))] if ordered else []),
    )


def front_partial(chunks, refl, before, last):
    shifts = list(chunks)
    ahead = [] if before is None else [before]

    def kernel(*refs):
        y_ref, out_ref, acc_ref = refs[-3], refs[-2], refs[-1]
        total = acc_ref if last else out_ref
        for k, d in enumerate(shifts):
            rows = y_ref[rows_at(ring_index(-d) * CAP, CAP), :]
            part = row_sums(refs[k][:CHUNK, :], rows)
            if k == 0 and before is not None:
                part = part + refs[len(shifts)][...]
            total[...] = part if k == 0 else total[...] + part
        if last:
            out_ref[...] = acc_ref[...].astype(BF16)

    return local_call(
        kernel,
        [in_vmem((COLS, REFL), BF16 if last else F32)],
        [*chunks.values(), *ahead, refl],
        scratch=[pltpu.VMEM((COLS, REFL), F32)],
    )[0]


def split_bf16(x):
    high = x.astype(BF16)
    return high, (x - high.astype(F32)).astype(BF16)


def fine_dot(a, b_high, b_low):
    a_high, a_low = split_bf16(a)
    dot = lambda u, v: jnp.dot(u, v, preferred_element_type=F32)
    return dot(a_high, b_high) + (dot(a_low, b_high) + dot(a_high, b_low))


def root_share(arrived, triangle):
    def kernel(x_ref, t_ref, out_ref):
        total = jnp.sum(x_ref[...].astype(F32), axis=0)
        rows = [jnp.concatenate([total[4 * c + j : 4 * c + j + 1] for j in range(4)], 1) for c in range(2)]
        both = jnp.concatenate(rows + [jnp.zeros((6, REFL), F32)], axis=0)
        coeffs = fine_dot(both, *split_bf16(t_ref[...]))
        chunk = jnp.concatenate(
            [coeffs[c : c + 1, 128 * j : 128 * (j + 1)] for c in range(2) for j in range(4)], 0
        )
        out_ref[...] = jnp.broadcast_to(chunk.astype(BF16)[None], out_ref.shape)

    return local_call(kernel, [in_vmem(arrived.shape)], [arrived, triangle])[0]


def front_share(arrived, high, low):
    def kernel(x_ref, high_ref, low_ref, out_ref):
        total = jnp.sum(x_ref[...].astype(F32), axis=0)
        coeffs = fine_dot(total, high_ref[...], low_ref[...]).astype(BF16)
        out_ref[...] = jnp.broadcast_to(coeffs[None], out_ref.shape)

    return local_call(kernel, [in_vmem(arrived.shape)], [arrived, high, low])[0]


LEAVING = in_vmem((CHUNK + FLAGS, COLS))


def leave(pick_panel, flags, pick_refl, ct_ref, out_ref):
    for i in range(CHUNK // TILE):
        update = times_coeffs(pick_refl(i), ct_ref[...])
        for b in range(TILE // BLOCK):
            p = i * (TILE // BLOCK) + b
            new = (pick_panel(p).astype(F32) - update[b * BLOCK : (b + 1) * BLOCK, :]) * flags[p]
            out_ref[p * BLOCK : (p + 1) * BLOCK, :] = new.astype(BF16)
    rows = flags + [jnp.zeros((FLAGS - CAP, COLS), F32)]
    out_ref[CHUNK:, :] = jnp.concatenate(rows, axis=0).astype(BF16)


def root_leave(shift, coeffs, panel, refl, table, first):
    def kernel(t_ref, c_ref, g_ref, y_ref, out_ref, *rest):
        if first:
            ct_ref, token_ref, tall_ref, ys_ref = rest
            token_ref[0] = 0
            tall_ref[...] = c_ref[...].astype(F32)
            for j in range(4):
                ct_ref[:, 128 * j : 128 * (j + 1)] = tall_ref[pl.ds(j, COLS, stride=4), :].astype(BF16)
        else:
            ct_ref, (ys_ref,) = c_ref, rest
        goal = ring_index(shift) * CAP
        at = [t_ref[goal + p] for p in range(CAP)]
        rows = [rows_at(jnp.maximum(k, 0)) for k in at]
        for p in range(CAP):
            ys_ref[p * BLOCK : (p + 1) * BLOCK, :] = y_ref[rows[p], :]
        flags = [jnp.broadcast_to(jnp.where(k >= 0, 1.0, 0.0).astype(F32), (1, COLS)) for k in at]
        leave(
            lambda p: g_ref[rows[p], :],
            flags,
            lambda i: ys_ref[i * TILE : (i + 1) * TILE, :],
            ct_ref,
            out_ref,
        )

    return local_call(
        kernel,
        [LEAVING] + ([in_vmem((COLS, REFL)), in_smem(1)] if first else []),
        [coeffs, panel, refl],
        [table],
        scratch=([pltpu.VMEM((COLS * 4, 128), F32)] if first else []) + [pltpu.VMEM((CHUNK, REFL), BF16)],
    )


def front_leave(shift, coeffs, chunks, ordered, table, first):
    def kernel(t_ref, c_ref, g0, g1, g2, g3, y_ref, out_ref, *rest):
        *token, gs_ref, flag_ref = rest
        for token_ref in token:
            token_ref[0] = 0
        for d, g_ref in enumerate((g0, g1, g2, g3)):
            flag_ref[d * FLAGS : (d + 1) * FLAGS, :] = g_ref[CHUNK:, :].astype(F32)
        goal = ring_index(shift) * CAP
        flags = []
        for p in range(CAP):
            block = t_ref[goal + p]
            chunk, place = ring_index(-(block // CAP)), block % CAP
            for d, g_ref in enumerate((g0, g1, g2, g3)):

                @pl.when(chunk == d)
                def _():
                    gs_ref[p * BLOCK : (p + 1) * BLOCK, :] = g_ref[rows_at(place), :]

            flags.append(flag_ref[pl.ds(chunk * FLAGS + place, 1), :])
        leave(
            lambda p: gs_ref[p * BLOCK : (p + 1) * BLOCK, :],
            flags,
            lambda i: y_ref[rows_at(goal + i * (TILE // BLOCK), TILE // BLOCK), :],
            c_ref,
            out_ref,
        )

    return local_call(
        kernel,
        [LEAVING] + ([in_smem(1)] if first else []),
        [coeffs, *chunks, ordered],
        [table],
        scratch=[pltpu.VMEM((CHUNK, COLS), BF16), pltpu.VMEM((FRONTS * FLAGS, COLS), F32)],
    )


def leaf_apply(coeffs, chunks, refl):
    per = CHUNK // TILE
    blocks = TILE // BLOCK

    def kernel(c_ref, g0, g1, g2, g3, y_ref, out_far, new_ref, sems):
        def leaving(d, i):
            return pltpu.make_async_copy(
                new_ref.at[pl.ds((d * per + i) * TILE, TILE)],
                out_far.at[rows_at(ring_index(-d) * CAP + i * blocks, blocks)],
                sems.at[d * per + i],
            )

        for d, g_ref in enumerate((g0, g1, g2, g3)):
            flags = g_ref[CHUNK:, :].astype(F32)
            for i in range(per):
                rows = rows_at(ring_index(-d) * CAP + i * blocks, blocks)
                update = times_coeffs(y_ref[rows, :], c_ref[...])
                for b in range(blocks):
                    p = i * blocks + b
                    old = g_ref[p * BLOCK : (p + 1) * BLOCK, :].astype(F32)
                    new = (old - update[b * BLOCK : (b + 1) * BLOCK, :]) * flags[p : p + 1, :]
                    at = d * CHUNK + p * BLOCK
                    new_ref[at : at + BLOCK, :] = new.astype(BF16)
                leaving(d, i).start()
        for d in range(FRONTS):
            for i in range(per):
                leaving(d, i).wait()

    return local_call(
        kernel,
        [(HBM, jax.ShapeDtypeStruct((FRONTS * CHUNK, COLS), BF16))],
        [coeffs, *chunks, refl],
        scratch=[pltpu.VMEM((FRONTS * CHUNK, COLS), BF16), DMA((FRONTS * per,))],
    )[0]


def all_to_all(x, axes):
    return lax.all_to_all(x, axes, 0, 0, tiled=True)


def shifted(x, d):
    return lax.ppermute(x, "front", [(i, (i + d) % FRONTS) for i in range(FRONTS)])


ORDER = (2, 1, 3)


def route(leaving):
    chunks = {}
    for d in ORDER + (0,):
        out = leaving(d)
        chunks[d] = shifted(out, d) if d else out
    return [chunks[d] for d in range(FRONTS)]


def front_level(chunks, refl, high, low):
    partial = None
    for group in ((0,), (2,), (1, 3)):
        partial = front_partial({d: chunks[d] for d in group}, refl, partial, group == (1, 3))
    arrived = all_to_all(partial.reshape(32, COLS // 32, REFL), ROWS)
    return all_to_all(front_share(arrived, high, low), ROWS).reshape(COLS, REFL)


def per_device(
    panel_g, refl_root, refl_mid, refl_leaf, tri_root, tri_mid, tri_leaf, route_root, route_mid
):
    panel = panel_g.reshape(-1, COLS)
    y_root, y_mid, y_leaf = (y.reshape(-1, REFL) for y in (refl_root, refl_mid, refl_leaf))

    partial, panel, y_root, root_table, mid_table = root_partial(
        panel, y_root, route_root.reshape(-1), route_mid.reshape(-1)
    )
    arrived = all_to_all(partial.reshape(128, 8, 128), ALL)
    coeffs = all_to_all(root_share(arrived, tri_root), ALL).reshape(COLS * 4, 128)
    token = None

    def from_root(d):
        nonlocal coeffs, token
        out = root_leave(d, coeffs, panel, y_root, root_table, token is None)
        if token is None:
            _, coeffs, token = out
        return out[0]

    chunks = route(from_root)
    y_mid, high, low, ordered = staged(y_mid, tri_mid[0], token, mid_table)
    coeffs = front_level(chunks, y_mid, high, low)
    arrived, token = chunks, None

    def from_middle(d):
        nonlocal token
        out = front_leave(d, coeffs, arrived, ordered, mid_table, token is None)
        if token is None:
            token = out[1]
        return out[0]

    chunks = route(from_middle)
    y_leaf, high, low = staged(y_leaf, tri_leaf[0], token, None)
    coeffs = front_level(chunks, y_leaf, high, low)
    out = leaf_apply(coeffs, chunks, y_leaf)
    return out.reshape(refl_leaf.shape[:3] + (COLS,))


def solution(mesh):
    finer = Mesh(
        mesh.devices.reshape(mesh.shape["front"], 4, 4, 2), ("front", "rows_0", "rows_1", "rows_2")
    )
    rows = P("front", ROWS, None, None)
    placed = (
        rows,
        rows,
        rows,
        rows,
        P(),
        P("front", None, None),
        P("front", None, None),
        P("front", ROWS, None),
        P("front", ROWS, None),
    )
    return jax.shard_map(
        per_device,
        mesh=finer,
        in_specs=placed,
        out_specs=rows,
        check_vma=False,
    )
```

```python
import jax
import jax.numpy as jnp
from jax import lax
from jax.experimental import pallas as pl
from jax.experimental.pallas import tpu as pltpu
from jax.sharding import Mesh
from jax.sharding import PartitionSpec as P


BLOCK = 128
FRONTS = 4
CAP = 8
COLS = 256
REFL = 512
CHUNK = CAP * BLOCK
FLAGS = 16
TILE = 512
ROWS = ("rows_0", "rows_1", "rows_2")
ALL = ("front",) + ROWS
F32 = jnp.float32
BF16 = jnp.bfloat16


def row_sums(panel, refl):
    return lax.dot_general(panel, refl, (((0,), (0,)), ((), ())), preferred_element_type=F32)


def times_coeffs(refl, coeffs_t):
    return lax.dot_general(refl, coeffs_t, (((1,), (1,)), ((), ())), preferred_element_type=F32)


VMEM = pl.BlockSpec(memory_space=pltpu.VMEM)
SMEM = pl.BlockSpec(memory_space=pltpu.SMEM)
HBM = pl.BlockSpec(memory_space=pltpu.MemorySpace.HBM)
DMA = pltpu.SemaphoreType.DMA


def local_call(kernel, outs, held=(), numbers=(), far=(), scratch=()):
    held = [pltpu.with_memory_space_constraint(a, pltpu.VMEM) for a in held]
    far = [pltpu.with_memory_space_constraint(a, pltpu.MemorySpace.HBM) for a in far]
    return pl.pallas_call(
        kernel,
        in_specs=[SMEM] * len(numbers) + [VMEM] * len(held) + [HBM] * len(far),
        out_specs=[spec for spec, _ in outs],
        out_shape=[shape for _, shape in outs],
        scratch_shapes=list(scratch),
        compiler_params=pltpu.CompilerParams(vmem_limit_bytes=12 << 20),
    )(*numbers, *held, *far)


def in_vmem(shape, dtype=BF16):
    return VMEM, pltpu.VMEM(shape, dtype)


def in_smem(count):
    return SMEM, jax.ShapeDtypeStruct((count,), jnp.int32)


def rows_at(block, count=1):
    return pl.ds(pl.multiple_of(block * BLOCK, BLOCK), count * BLOCK)


def root_partial(panel, refl, route_root, route_mid):
    rows = panel.shape[0]
    steps = rows // TILE
    slots = FRONTS * CAP

    def place_blocks(route_ref, table_ref, seen_ref):
        for goal in range(FRONTS):
            seen_ref[goal] = 0

        def body(i, _):
            goal = route_ref[i]
            table_ref[goal * CAP + seen_ref[goal]] = i
            seen_ref[goal] = seen_ref[goal] + 1
            return 0

        lax.fori_loop(0, route_ref.shape[0], body, 0)

    def kernel(
        g_far, y_far, r0_far, r1_far, out_ref, g_ref, y_ref, t0_ref, t1_ref, tall_ref, acc_ref, seen_ref, r0_ref, r1_ref, sems, route_sems
    ):
        routes = [
            pltpu.make_async_copy(r0_far, r0_ref, route_sems.at[0]),
            pltpu.make_async_copy(r1_far, r1_ref, route_sems.at[1]),
        ]
        for copy in routes:
            copy.start()

        def copies(i):
            at = pl.ds(i * TILE, TILE)
            return [
                pltpu.make_async_copy(far.at[at], near.at[at], sems.at[k, i])
                for k, (far, near) in enumerate(((y_far, y_ref), (g_far, g_ref)))
            ]

        for i in range(steps):
            for copy in copies(i):
                copy.start()
        for i in range(slots):
            t0_ref[i] = -1
        for copy in routes:
            copy.wait()
        place_blocks(r0_ref, t0_ref, seen_ref)
        place_blocks(r1_ref, t1_ref, seen_ref)
        for i in range(steps):
            for copy in copies(i):
                copy.wait()
            at = slice(i * TILE, (i + 1) * TILE)
            part = row_sums(g_ref[at, :], y_ref[at, :])
            acc_ref[...] = part if i == 0 else acc_ref[...] + part
        for j in range(4):
            tall_ref[pl.ds(j, COLS, stride=4), :] = acc_ref[:, 128 * j : 128 * (j + 1)]
        out_ref[...] = tall_ref[...].astype(BF16)

    return local_call(
        kernel,
        [in_vmem((COLS * 4, 128)), in_vmem((rows, COLS)), in_vmem((rows, REFL))]
        + [in_smem(slots), in_smem(slots)],
        far=[panel, refl, route_root, route_mid],
        scratch=[
            pltpu.VMEM((COLS * 4, 128), F32),
            pltpu.VMEM((COLS, REFL), F32),
            pltpu.SMEM((FRONTS,), jnp.int32),
            pltpu.SMEM(route_root.shape, jnp.int32),
            pltpu.SMEM(route_mid.shape, jnp.int32),
            DMA((2, steps)),
            DMA((2,)),
        ],
    )


def ring_index(shift):
    return jnp.bitwise_and(lax.axis_index("front") + shift, FRONTS - 1)


def staged(refl, triangle, after, table):
    ordered = table is not None
    slots = FRONTS * CAP

    def kernel(*refs):
        if ordered:
            _, table_ref, y_far, t_far, order_ref, v_ref, y_ref, t_ref, sems, order_sems = refs
        else:
            _, y_far, t_far, y_ref, v_ref, t_ref, sems = refs
        triangle_copy = pltpu.make_async_copy(t_far, t_ref, sems.at[0])
        refl_copy = pltpu.make_async_copy(y_far, y_ref, sems.at[1])
        triangle_copy.start()
        refl_copy.start()
        blocks = []
        if ordered:
            blocks = [
                pltpu.make_async_copy(
                    y_far.at[rows_at(table_ref[k])],
                    order_ref.at[pl.ds(k * BLOCK, BLOCK)],
                    order_sems.at[k],
                )
                for k in range(slots)
            ]
            for copy in blocks:
                copy.start()
        triangle_copy.wait()
        refl_copy.wait()
        high, low = split_bf16(t_ref[...])
        for i in range(slots * BLOCK // TILE):
            at = slice(i * TILE, (i + 1) * TILE)
            dot = lambda t: jnp.dot(y_ref[at, :], t, preferred_element_type=F32)
            v_ref[at, :] = (dot(high) + dot(low)).astype(BF16)
        for copy in blocks:
            copy.wait()

    held = [pltpu.VMEM(refl.shape, BF16)] if ordered else []
    return local_call(
        kernel,
        [in_vmem(refl.shape)] * 2,
        numbers=[after] + ([table] if ordered else []),
        far=[refl, triangle],
        scratch=held + [pltpu.VMEM((REFL, REFL), F32), DMA((2,))] + ([DMA((slots,))] if ordered else []),
    )


def front_partial(chunks, refl, before, last):
    shifts = list(chunks)
    ahead = [] if before is None else [before]

    def kernel(*refs):
        y_ref, out_ref, acc_ref = refs[-3], refs[-2], refs[-1]
        total = acc_ref if last else out_ref
        for k, d in enumerate(shifts):
            rows = y_ref[rows_at(ring_index(-d) * CAP, CAP), :]
            part = row_sums(refs[k][:CHUNK, :], rows)
            if k == 0 and before is not None:
                part = part + refs[len(shifts)][...]
            total[...] = part if k == 0 else total[...] + part
        if last:
            out_ref[...] = acc_ref[...].astype(BF16)

    return local_call(
        kernel,
        [in_vmem((COLS, REFL), BF16 if last else F32)],
        [*chunks.values(), *ahead, refl],
        scratch=[pltpu.VMEM((COLS, REFL), F32)],
    )[0]


def split_bf16(x):
    high = x.astype(BF16)
    return high, (x - high.astype(F32)).astype(BF16)


def fine_dot(a, b_high, b_low):
    a_high, a_low = split_bf16(a)
    dot = lambda u, v: jnp.dot(u, v, preferred_element_type=F32)
    return dot(a_high, b_high) + (dot(a_low, b_high) + dot(a_high, b_low))


def root_share(arrived, triangle):
    def kernel(x_ref, t_ref, out_ref):
        total = jnp.sum(x_ref[...].astype(F32), axis=0)
        rows = [jnp.concatenate([total[4 * c + j : 4 * c + j + 1] for j in range(4)], 1) for c in range(2)]
        both = jnp.concatenate(rows + [jnp.zeros((6, REFL), F32)], axis=0)
        coeffs = fine_dot(both, *split_bf16(t_ref[...]))
        chunk = jnp.concatenate(
            [coeffs[c : c + 1, 128 * j : 128 * (j + 1)] for c in range(2) for j in range(4)], 0
        )
        out_ref[...] = jnp.broadcast_to(chunk.astype(BF16)[None], out_ref.shape)

    return local_call(kernel, [in_vmem(arrived.shape)], [arrived, triangle])[0]


def front_share(arrived):
    def kernel(x_ref, out_ref):
        total = jnp.sum(x_ref[...].astype(F32), axis=0).astype(BF16)
        out_ref[...] = jnp.broadcast_to(total[None], out_ref.shape)

    return local_call(kernel, [in_vmem(arrived.shape)], [arrived])[0]


LEAVING = in_vmem((CHUNK + FLAGS, COLS))


def leave(pick_panel, flags, pick_refl, ct_ref, out_ref):
    for i in range(CHUNK // TILE):
        update = times_coeffs(pick_refl(i), ct_ref[...])
        for b in range(TILE // BLOCK):
            p = i * (TILE // BLOCK) + b
            new = (pick_panel(p).astype(F32) - update[b * BLOCK : (b + 1) * BLOCK, :]) * flags[p]
            out_ref[p * BLOCK : (p + 1) * BLOCK, :] = new.astype(BF16)
    rows = flags + [jnp.zeros((FLAGS - CAP, COLS), F32)]
    out_ref[CHUNK:, :] = jnp.concatenate(rows, axis=0).astype(BF16)


def root_leave(shift, coeffs, panel, refl, table, first):
    def kernel(t_ref, c_ref, g_ref, y_ref, out_ref, *rest):
        if first:
            ct_ref, token_ref, tall_ref, ys_ref = rest
            token_ref[0] = 0
            tall_ref[...] = c_ref[...].astype(F32)
            for j in range(4):
                ct_ref[:, 128 * j : 128 * (j + 1)] = tall_ref[pl.ds(j, COLS, stride=4), :].astype(BF16)
        else:
            ct_ref, (ys_ref,) = c_ref, rest
        goal = ring_index(shift) * CAP
        at = [t_ref[goal + p] for p in range(CAP)]
        rows = [rows_at(jnp.maximum(k, 0)) for k in at]
        for p in range(CAP):
            ys_ref[p * BLOCK : (p + 1) * BLOCK, :] = y_ref[rows[p], :]
        flags = [jnp.broadcast_to(jnp.where(k >= 0, 1.0, 0.0).astype(F32), (1, COLS)) for k in at]
        leave(
            lambda p: g_ref[rows[p], :],
            flags,
            lambda i: ys_ref[i * TILE : (i + 1) * TILE, :],
            ct_ref,
            out_ref,
        )

    return local_call(
        kernel,
        [LEAVING] + ([in_vmem((COLS, REFL)), in_smem(1)] if first else []),
        [coeffs, panel, refl],
        [table],
        scratch=([pltpu.VMEM((COLS * 4, 128), F32)] if first else []) + [pltpu.VMEM((CHUNK, REFL), BF16)],
    )


def front_leave(shift, coeffs, chunks, ordered, table, first):
    def kernel(t_ref, c_ref, g0, g1, g2, g3, y_ref, out_ref, *rest):
        *token, gs_ref, flag_ref = rest
        for token_ref in token:
            token_ref[0] = 0
        for d, g_ref in enumerate((g0, g1, g2, g3)):
            flag_ref[d * FLAGS : (d + 1) * FLAGS, :] = g_ref[CHUNK:, :].astype(F32)
        goal = ring_index(shift) * CAP
        flags = []
        for p in range(CAP):
            block = t_ref[goal + p]
            chunk, place = ring_index(-(block // CAP)), block % CAP
            for d, g_ref in enumerate((g0, g1, g2, g3)):

                @pl.when(chunk == d)
                def _():
                    gs_ref[p * BLOCK : (p + 1) * BLOCK, :] = g_ref[rows_at(place), :]

            flags.append(flag_ref[pl.ds(chunk * FLAGS + place, 1), :])
        leave(
            lambda p: gs_ref[p * BLOCK : (p + 1) * BLOCK, :],
            flags,
            lambda i: y_ref[rows_at(goal + i * (TILE // BLOCK), TILE // BLOCK), :],
            c_ref,
            out_ref,
        )

    return local_call(
        kernel,
        [LEAVING] + ([in_smem(1)] if first else []),
        [coeffs, *chunks, ordered],
        [table],
        scratch=[pltpu.VMEM((CHUNK, COLS), BF16), pltpu.VMEM((FRONTS * FLAGS, COLS), F32)],
    )


def leaf_apply(coeffs, chunks, refl):
    per = CHUNK // TILE
    blocks = TILE // BLOCK

    def kernel(c_ref, g0, g1, g2, g3, y_ref, out_far, new_ref, sems):
        def leaving(d, i):
            return pltpu.make_async_copy(
                new_ref.at[pl.ds((d * per + i) * TILE, TILE)],
                out_far.at[rows_at(ring_index(-d) * CAP + i * blocks, blocks)],
                sems.at[d * per + i],
            )

        for d, g_ref in enumerate((g0, g1, g2, g3)):
            flags = g_ref[CHUNK:, :].astype(F32)
            for i in range(per):
                rows = rows_at(ring_index(-d) * CAP + i * blocks, blocks)
                update = times_coeffs(y_ref[rows, :], c_ref[...])
                for b in range(blocks):
                    p = i * blocks + b
                    old = g_ref[p * BLOCK : (p + 1) * BLOCK, :].astype(F32)
                    new = (old - update[b * BLOCK : (b + 1) * BLOCK, :]) * flags[p : p + 1, :]
                    at = d * CHUNK + p * BLOCK
                    new_ref[at : at + BLOCK, :] = new.astype(BF16)
                leaving(d, i).start()
        for d in range(FRONTS):
            for i in range(per):
                leaving(d, i).wait()

    return local_call(
        kernel,
        [(HBM, jax.ShapeDtypeStruct((FRONTS * CHUNK, COLS), BF16))],
        [coeffs, *chunks, refl],
        scratch=[pltpu.VMEM((FRONTS * CHUNK, COLS), BF16), DMA((FRONTS * per,))],
    )[0]


def all_to_all(x, axes):
    return lax.all_to_all(x, axes, 0, 0, tiled=True)


def shifted(x, d):
    return lax.ppermute(x, "front", [(i, (i + d) % FRONTS) for i in range(FRONTS)])


ORDER = (2, 1, 3)


def route(leaving):
    chunks = {}
    for d in ORDER + (0,):
        out = leaving(d)
        chunks[d] = shifted(out, d) if d else out
    return [chunks[d] for d in range(FRONTS)]


def front_level(chunks, refl):
    partial = None
    for group in ((0,), (2,), (1, 3)):
        partial = front_partial({d: chunks[d] for d in group}, refl, partial, group == (1, 3))
    arrived = all_to_all(partial.reshape(32, COLS // 32, REFL), ROWS)
    return all_to_all(front_share(arrived), ROWS).reshape(COLS, REFL)


def per_device(
    panel_g, refl_root, refl_mid, refl_leaf, tri_root, tri_mid, tri_leaf, route_root, route_mid
):
    panel = panel_g.reshape(-1, COLS)
    y_root, y_mid, y_leaf = (y.reshape(-1, REFL) for y in (refl_root, refl_mid, refl_leaf))

    partial, panel, y_root, root_table, mid_table = root_partial(
        panel, y_root, route_root.reshape(-1), route_mid.reshape(-1)
    )
    arrived = all_to_all(partial.reshape(128, 8, 128), ALL)
    coeffs = all_to_all(root_share(arrived, tri_root), ALL).reshape(COLS * 4, 128)
    token = None

    def from_root(d):
        nonlocal coeffs, token
        out = root_leave(d, coeffs, panel, y_root, root_table, token is None)
        if token is None:
            _, coeffs, token = out
        return out[0]

    chunks = route(from_root)
    ordered, v_mid = staged(y_mid, tri_mid[0], token, mid_table)
    coeffs = front_level(chunks, v_mid)
    arrived, token = chunks, None

    def from_middle(d):
        nonlocal token
        out = front_leave(d, coeffs, arrived, ordered, mid_table, token is None)
        if token is None:
            token = out[1]
        return out[0]

    chunks = route(from_middle)
    y_leaf, v_leaf = staged(y_leaf, tri_leaf[0], token, None)
    coeffs = front_level(chunks, v_leaf)
    out = leaf_apply(coeffs, chunks, y_leaf)
    return out.reshape(refl_leaf.shape[:3] + (COLS,))


def solution(mesh):
    finer = Mesh(
        mesh.devices.reshape(mesh.shape["front"], 4, 4, 2), ("front", "rows_0", "rows_1", "rows_2")
    )
    rows = P("front", ROWS, None, None)
    placed = (
        rows,
        rows,
        rows,
        rows,
        P(),
        P("front", None, None),
        P("front", None, None),
        P("front", ROWS, None),
        P("front", ROWS, None),
    )
    return jax.shard_map(
        per_device,
        mesh=finer,
        in_specs=placed,
        out_specs=rows,
        check_vma=False,
    )
```

```python
import jax
import jax.numpy as jnp
from jax import lax
from jax.experimental import pallas as pl
from jax.experimental.pallas import tpu as pltpu
from jax.sharding import Mesh
from jax.sharding import PartitionSpec as P


BLOCK = 128
FRONTS = 4
CAP = 8
COLS = 256
REFL = 512
CHUNK = CAP * BLOCK
FLAGS = 16
TILE = 512
ROWS = ("rows_0", "rows_1", "rows_2")
ALL = ("front",) + ROWS
F32 = jnp.float32
BF16 = jnp.bfloat16


def row_sums(panel, refl):
    return lax.dot_general(panel, refl, (((0,), (0,)), ((), ())), preferred_element_type=F32)


def times_coeffs(refl, coeffs_t):
    return lax.dot_general(refl, coeffs_t, (((1,), (1,)), ((), ())), preferred_element_type=F32)


VMEM = pl.BlockSpec(memory_space=pltpu.VMEM)
SMEM = pl.BlockSpec(memory_space=pltpu.SMEM)
HBM = pl.BlockSpec(memory_space=pltpu.MemorySpace.HBM)
DMA = pltpu.SemaphoreType.DMA


def local_call(kernel, outs, held=(), numbers=(), far=(), scratch=()):
    held = [pltpu.with_memory_space_constraint(a, pltpu.VMEM) for a in held]
    far = [pltpu.with_memory_space_constraint(a, pltpu.MemorySpace.HBM) for a in far]
    return pl.pallas_call(
        kernel,
        in_specs=[SMEM] * len(numbers) + [VMEM] * len(held) + [HBM] * len(far),
        out_specs=[spec for spec, _ in outs],
        out_shape=[shape for _, shape in outs],
        scratch_shapes=list(scratch),
        compiler_params=pltpu.CompilerParams(vmem_limit_bytes=12 << 20),
    )(*numbers, *held, *far)


def in_vmem(shape, dtype=BF16):
    return VMEM, pltpu.VMEM(shape, dtype)


def in_smem(count):
    return SMEM, jax.ShapeDtypeStruct((count,), jnp.int32)


def rows_at(block, count=1):
    return pl.ds(pl.multiple_of(block * BLOCK, BLOCK), count * BLOCK)


def root_partial(panel, refl, route_root, route_mid):
    rows = panel.shape[0]
    steps = rows // TILE
    slots = FRONTS * CAP

    def place_blocks(route_ref, table_ref, seen_ref):
        for goal in range(FRONTS):
            seen_ref[goal] = 0

        def body(i, _):
            goal = route_ref[i]
            table_ref[goal * CAP + seen_ref[goal]] = i
            seen_ref[goal] = seen_ref[goal] + 1
            return 0

        lax.fori_loop(0, route_ref.shape[0], body, 0)

    def kernel(
        g_far, y_far, r0_far, r1_far, out_ref, g_ref, y_ref, t0_ref, t1_ref, tall_ref, acc_ref, seen_ref, r0_ref, r1_ref, sems, route_sems
    ):
        routes = [
            pltpu.make_async_copy(r0_far, r0_ref, route_sems.at[0]),
            pltpu.make_async_copy(r1_far, r1_ref, route_sems.at[1]),
        ]
        for copy in routes:
            copy.start()

        def copies(i):
            at = pl.ds(i * TILE, TILE)
            return [
                pltpu.make_async_copy(far.at[at], near.at[at], sems.at[k, i])
                for k, (far, near) in enumerate(((y_far, y_ref), (g_far, g_ref)))
            ]

        for i in range(steps):
            for copy in copies(i):
                copy.start()
        for i in range(slots):
            t0_ref[i] = -1
        for copy in routes:
            copy.wait()
        place_blocks(r0_ref, t0_ref, seen_ref)
        place_blocks(r1_ref, t1_ref, seen_ref)
        for i in range(steps):
            for copy in copies(i):
                copy.wait()
            at = slice(i * TILE, (i + 1) * TILE)
            part = row_sums(g_ref[at, :], y_ref[at, :])
            acc_ref[...] = part if i == 0 else acc_ref[...] + part
        for j in range(4):
            tall_ref[pl.ds(j, COLS, stride=4), :] = acc_ref[:, 128 * j : 128 * (j + 1)]
        out_ref[...] = tall_ref[...].astype(BF16)

    return local_call(
        kernel,
        [in_vmem((COLS * 4, 128)), in_vmem((rows, COLS)), in_vmem((rows, REFL))]
        + [in_smem(slots), in_smem(slots)],
        far=[panel, refl, route_root, route_mid],
        scratch=[
            pltpu.VMEM((COLS * 4, 128), F32),
            pltpu.VMEM((COLS, REFL), F32),
            pltpu.SMEM((FRONTS,), jnp.int32),
            pltpu.SMEM(route_root.shape, jnp.int32),
            pltpu.SMEM(route_mid.shape, jnp.int32),
            DMA((2, steps)),
            DMA((2,)),
        ],
    )


def ring_index(shift):
    return jnp.bitwise_and(lax.axis_index("front") + shift, FRONTS - 1)


def staged(refl, triangle, after, table):
    ordered = table is not None
    slots = FRONTS * CAP

    def kernel(*refs):
        if ordered:
            _, table_ref, y_far, t_far, order_ref, v_ref, y_ref, t_ref, sems, order_sems = refs
        else:
            _, y_far, t_far, y_ref, v_ref, t_ref, sems = refs
        triangle_copy = pltpu.make_async_copy(t_far, t_ref, sems.at[0])
        refl_copy = pltpu.make_async_copy(y_far, y_ref, sems.at[1])
        triangle_copy.start()
        refl_copy.start()
        blocks = []
        if ordered:
            blocks = [
                pltpu.make_async_copy(
                    y_far.at[rows_at(table_ref[k])],
                    order_ref.at[pl.ds(k * BLOCK, BLOCK)],
                    order_sems.at[k],
                )
                for k in range(slots)
            ]
            for copy in blocks:
                copy.start()
        triangle_copy.wait()
        refl_copy.wait()
        high, low = split_bf16(t_ref[...])
        for i in range(slots * BLOCK // TILE):
            at = slice(i * TILE, (i + 1) * TILE)
            dot = lambda t: jnp.dot(y_ref[at, :], t, preferred_element_type=F32)
            v_ref[at, :] = (dot(high) + dot(low)).astype(BF16)
        for copy in blocks:
            copy.wait()

    held = [pltpu.VMEM(refl.shape, BF16)] if ordered else []
    return local_call(
        kernel,
        [in_vmem(refl.shape)] * 2,
        numbers=[after] + ([table] if ordered else []),
        far=[refl, triangle],
        scratch=held + [pltpu.VMEM((REFL, REFL), F32), DMA((2,))] + ([DMA((slots,))] if ordered else []),
    )


def front_partial(chunks, refl, before, last):
    shifts = list(chunks)
    ahead = [] if before is None else [before]

    def kernel(*refs):
        y_ref, out_ref, acc_ref = refs[-3], refs[-2], refs[-1]
        total = acc_ref if last else out_ref
        for k, d in enumerate(shifts):
            rows = y_ref[rows_at(ring_index(-d) * CAP, CAP), :]
            part = row_sums(refs[k][:CHUNK, :], rows)
            if k == 0 and before is not None:
                part = part + refs[len(shifts)][...]
            total[...] = part if k == 0 else total[...] + part
        if last:
            out_ref[...] = acc_ref[...].astype(BF16)

    return local_call(
        kernel,
        [in_vmem((COLS, REFL), BF16 if last else F32)],
        [*chunks.values(), *ahead, refl],
        scratch=[pltpu.VMEM((COLS, REFL), F32)],
    )[0]


def split_bf16(x):
    high = x.astype(BF16)
    return high, (x - high.astype(F32)).astype(BF16)


def fine_dot(a, b_high, b_low):
    a_high, a_low = split_bf16(a)
    dot = lambda u, v: jnp.dot(u, v, preferred_element_type=F32)
    return dot(a_high, b_high) + (dot(a_low, b_high) + dot(a_high, b_low))


def root_share(arrived, triangle):
    def kernel(x_ref, t_ref, out_ref):
        total = jnp.sum(x_ref[...].astype(F32), axis=0)
        rows = [jnp.concatenate([total[4 * c + j : 4 * c + j + 1] for j in range(4)], 1) for c in range(2)]
        both = jnp.concatenate(rows + [jnp.zeros((6, REFL), F32)], axis=0)
        coeffs = fine_dot(both, *split_bf16(t_ref[...]))
        chunk = jnp.concatenate(
            [coeffs[c : c + 1, 128 * j : 128 * (j + 1)] for c in range(2) for j in range(4)], 0
        )
        out_ref[...] = jnp.broadcast_to(chunk.astype(BF16)[None], out_ref.shape)

    return local_call(kernel, [in_vmem(arrived.shape)], [arrived, triangle])[0]


def front_share(arrived):
    def kernel(x_ref, out_ref):
        total = jnp.sum(x_ref[...].astype(F32), axis=0).astype(BF16)
        out_ref[...] = jnp.broadcast_to(total[None], out_ref.shape)

    return local_call(kernel, [in_vmem(arrived.shape)], [arrived])[0]


LEAVING = in_vmem((CHUNK + FLAGS, COLS))


def leave(pick_panel, flags, pick_refl, ct_ref, out_ref):
    for i in range(CHUNK // TILE):
        update = times_coeffs(pick_refl(i), ct_ref[...])
        for b in range(TILE // BLOCK):
            p = i * (TILE // BLOCK) + b
            new = (pick_panel(p).astype(F32) - update[b * BLOCK : (b + 1) * BLOCK, :]) * flags[p]
            out_ref[p * BLOCK : (p + 1) * BLOCK, :] = new.astype(BF16)
    rows = flags + [jnp.zeros((FLAGS - CAP, COLS), F32)]
    out_ref[CHUNK:, :] = jnp.concatenate(rows, axis=0).astype(BF16)


def root_leave(shift, coeffs, panel, refl, table, first):
    def kernel(t_ref, c_ref, g_ref, y_ref, out_ref, *rest):
        if first:
            ct_ref, token_ref, tall_ref, ys_ref = rest
            token_ref[0] = 0
            tall_ref[...] = c_ref[...].astype(F32)
            for j in range(4):
                ct_ref[:, 128 * j : 128 * (j + 1)] = tall_ref[pl.ds(j, COLS, stride=4), :].astype(BF16)
        else:
            ct_ref, (ys_ref,) = c_ref, rest
        goal = ring_index(shift) * CAP
        at = [t_ref[goal + p] for p in range(CAP)]
        rows = [rows_at(jnp.maximum(k, 0)) for k in at]
        for p in range(CAP):
            ys_ref[p * BLOCK : (p + 1) * BLOCK, :] = y_ref[rows[p], :]
        flags = [jnp.broadcast_to(jnp.where(k >= 0, 1.0, 0.0).astype(F32), (1, COLS)) for k in at]
        leave(
            lambda p: g_ref[rows[p], :],
            flags,
            lambda i: ys_ref[i * TILE : (i + 1) * TILE, :],
            ct_ref,
            out_ref,
        )

    return local_call(
        kernel,
        [LEAVING] + ([in_vmem((COLS, REFL)), in_smem(1)] if first else []),
        [coeffs, panel, refl],
        [table],
        scratch=([pltpu.VMEM((COLS * 4, 128), F32)] if first else []) + [pltpu.VMEM((CHUNK, REFL), BF16)],
    )


def front_leave(shift, coeffs, chunks, ordered, table, first):
    def kernel(t_ref, c_ref, g0, g1, g2, g3, y_ref, out_ref, *rest):
        *token, gs_ref, flag_ref = rest
        for token_ref in token:
            token_ref[0] = 0
        for d, g_ref in enumerate((g0, g1, g2, g3)):
            flag_ref[d * FLAGS : (d + 1) * FLAGS, :] = g_ref[CHUNK:, :].astype(F32)
        goal = ring_index(shift) * CAP
        flags = []
        for p in range(CAP):
            block = t_ref[goal + p]
            chunk, place = ring_index(-(block // CAP)), block % CAP
            for d, g_ref in enumerate((g0, g1, g2, g3)):

                @pl.when(chunk == d)
                def _():
                    gs_ref[p * BLOCK : (p + 1) * BLOCK, :] = g_ref[rows_at(place), :]

            flags.append(flag_ref[pl.ds(chunk * FLAGS + place, 1), :])
        leave(
            lambda p: gs_ref[p * BLOCK : (p + 1) * BLOCK, :],
            flags,
            lambda i: y_ref[rows_at(goal + i * (TILE // BLOCK), TILE // BLOCK), :],
            c_ref,
            out_ref,
        )

    return local_call(
        kernel,
        [LEAVING] + ([in_smem(1)] if first else []),
        [coeffs, *chunks, ordered],
        [table],
        scratch=[pltpu.VMEM((CHUNK, COLS), BF16), pltpu.VMEM((FRONTS * FLAGS, COLS), F32)],
    )


def leaf_apply(coeffs, chunks, refl):
    per = CHUNK // TILE
    blocks = TILE // BLOCK

    def kernel(c_ref, g0, g1, g2, g3, y_ref, out_far, new_ref, sems):
        def leaving(d):
            return pltpu.make_async_copy(
                new_ref.at[pl.ds(d * CHUNK, CHUNK)],
                out_far.at[rows_at(ring_index(-d) * CAP, CAP)],
                sems.at[d],
            )

        for d, g_ref in enumerate((g0, g1, g2, g3)):
            flags = g_ref[CHUNK:, :].astype(F32)
            for i in range(per):
                rows = rows_at(ring_index(-d) * CAP + i * blocks, blocks)
                update = times_coeffs(y_ref[rows, :], c_ref[...])
                for b in range(blocks):
                    p = i * blocks + b
                    old = g_ref[p * BLOCK : (p + 1) * BLOCK, :].astype(F32)
                    new = (old - update[b * BLOCK : (b + 1) * BLOCK, :]) * flags[p : p + 1, :]
                    at = d * CHUNK + p * BLOCK
                    new_ref[at : at + BLOCK, :] = new.astype(BF16)
            leaving(d).start()
        for d in range(FRONTS):
            leaving(d).wait()

    return local_call(
        kernel,
        [(HBM, jax.ShapeDtypeStruct((FRONTS * CHUNK, COLS), BF16))],
        [coeffs, *chunks, refl],
        scratch=[pltpu.VMEM((FRONTS * CHUNK, COLS), BF16), DMA((FRONTS,))],
    )[0]


def all_to_all(x, axes):
    return lax.all_to_all(x, axes, 0, 0, tiled=True)


def shifted(x, d):
    return lax.ppermute(x, "front", [(i, (i + d) % FRONTS) for i in range(FRONTS)])


ORDER = (2, 1, 3)


def route(leaving):
    chunks = {}
    for d in ORDER + (0,):
        out = leaving(d)
        chunks[d] = shifted(out, d) if d else out
    return [chunks[d] for d in range(FRONTS)]


def front_level(chunks, refl):
    partial = None
    for group in ((0,), (2,), (1, 3)):
        partial = front_partial({d: chunks[d] for d in group}, refl, partial, group == (1, 3))
    arrived = all_to_all(partial.reshape(32, COLS // 32, REFL), ROWS)
    return all_to_all(front_share(arrived), ROWS).reshape(COLS, REFL)


def per_device(
    panel_g, refl_root, refl_mid, refl_leaf, tri_root, tri_mid, tri_leaf, route_root, route_mid
):
    panel = panel_g.reshape(-1, COLS)
    y_root, y_mid, y_leaf = (y.reshape(-1, REFL) for y in (refl_root, refl_mid, refl_leaf))

    partial, panel, y_root, root_table, mid_table = root_partial(
        panel, y_root, route_root.reshape(-1), route_mid.reshape(-1)
    )
    arrived = all_to_all(partial.reshape(128, 8, 128), ALL)
    coeffs = all_to_all(root_share(arrived, tri_root), ALL).reshape(COLS * 4, 128)
    token = None

    def from_root(d):
        nonlocal coeffs, token
        out = root_leave(d, coeffs, panel, y_root, root_table, token is None)
        if token is None:
            _, coeffs, token = out
        return out[0]

    chunks = route(from_root)
    ordered, v_mid = staged(y_mid, tri_mid[0], token, mid_table)
    coeffs = front_level(chunks, v_mid)
    arrived, token = chunks, None

    def from_middle(d):
        nonlocal token
        out = front_leave(d, coeffs, arrived, ordered, mid_table, token is None)
        if token is None:
            token = out[1]
        return out[0]

    chunks = route(from_middle)
    y_leaf, v_leaf = staged(y_leaf, tri_leaf[0], token, None)
    coeffs = front_level(chunks, v_leaf)
    out = leaf_apply(coeffs, chunks, y_leaf)
    return out.reshape(refl_leaf.shape[:3] + (COLS,))


def solution(mesh):
    finer = Mesh(
        mesh.devices.reshape(mesh.shape["front"], 4, 4, 2), ("front", "rows_0", "rows_1", "rows_2")
    )
    rows = P("front", ROWS, None, None)
    placed = (
        rows,
        rows,
        rows,
        rows,
        P(),
        P("front", None, None),
        P("front", None, None),
        P("front", ROWS, None),
        P("front", ROWS, None),
    )
    return jax.shard_map(
        per_device,
        mesh=finer,
        in_specs=placed,
        out_specs=rows,
        check_vma=False,
    )
```
